32 devices in a mesh: group: 2 (over x), sample: 16 (over z, y, core).
Axes of the slice: x: 2, y: 2, z: 4, core: 2. Of those that a mesh axis runs over, the one named last changes fastest.
Arguments:
- queries: bfloat16 [32, 3, 64, 128], P(('group', 'sample')), parts along dimension 0, may hold values from -150 to 150
- prefix_keys: bfloat16 [4096, 8, 128], P(('group', 'sample')), parts along dimension 0, may hold values from -5 to 5
- prefix_values: bfloat16 [4096, 8, 128], P(('group', 'sample')), parts along dimension 0, may hold values from -6 to 6
- suffix_keys: bfloat16 [32, 1024, 8, 128], P(('group', 'sample')), parts along dimension 0, may hold values from -7 to 7
- suffix_values: bfloat16 [32, 1024, 8, 128], P(('group', 'sample')), parts along dimension 0, may hold values from -6 to 6
- suffix_lengths: int32 [32], P(('group', 'sample')), parts along dimension 0, may hold values from 0 to 1024, as said below
- new_keys: bfloat16 [32, 3, 8, 128], P(('group', 'sample')), parts along dimension 0, may hold values from -5 to 5
- new_values: bfloat16 [32, 3, 8, 128], P(('group', 'sample')), parts along dimension 0, may hold values from -6 to 6
Outputs:
- attention: float32 [32, 3, 64, 128], P(('group', 'sample')), parts along dimension 0
The draws below stay inside these ranges and needn't reach their ends.
There are 2 independent parts, one for each index of `group`. The reference program is written for one: setup_inputs(seed, part) draws one part's arguments, and reference() takes and returns one part's arrays. A program takes and returns all parts, laid end to end along the dimension named above; each array names one. Nothing has to cross between parts.
Inputs may be any that keep to these rules, and one draw needn't show every extreme that they name: `suffix_lengths`: some sample of every group has exactly 1024 generated tokens.
All inputs are finite; a program needn't handle non-finite values.
Results may differ from the reference program's by a relative error of at most 0.00042.
Values may be sent and summed in bfloat16 or wider, within the bound.
A program may use at most 128 MiB of HBM per device.

```python
import jax
import jax.numpy as jnp
from jax import lax

H = 64
KVH = 8
HD = 128
STEPS = 3
PRE_DEV = 128
SUF = 1024
SAMPLES = 16
PREFIX = 2048
N_SAMPLE = 16


def shared_draw(key):
    prompt_keys = jax.random.truncated_normal(jax.random.fold_in(key, 11), -5.0, 5.0, (PREFIX, KVH, HD), jnp.float32)
    fresh_keys = jax.random.truncated_normal(jax.random.fold_in(key, 12), -5.0, 5.0, (SAMPLES, STEPS, KVH, HD), jnp.float32)
    noise = 3.0 * jax.random.normal(jax.random.fold_in(key, 13), (SAMPLES, STEPS, H, HD), jnp.float32)
    query_draw = noise + 1.4 * jnp.repeat(fresh_keys, H // KVH, axis=2)
    query_draw = jnp.clip(query_draw, -150.0, 150.0)
    return (prompt_keys, fresh_keys, query_draw)


def draw_queries(key, part):
    return shared_draw(key)[2].astype(jnp.bfloat16)


def draw_prefix_keys(key, part):
    return shared_draw(key)[0].astype(jnp.bfloat16)


def draw_new_keys(key, part):
    return shared_draw(key)[1].astype(jnp.bfloat16)


def draw_suffix_lengths(key, part):
    first_draw = jax.random.randint(jax.random.fold_in(key, 21), (SAMPLES,), 0, SUF + 1, jnp.int32)
    second_draw = jax.random.randint(jax.random.fold_in(key, 22), (SAMPLES,), 0, SUF + 1, jnp.int32)
    lengths = first_draw * second_draw // SUF
    chosen = jax.random.randint(jax.random.fold_in(key, 23), (), 0, SAMPLES, jnp.int32)
    return jnp.where(jnp.arange(SAMPLES, dtype=jnp.int32) == chosen, SUF, lengths).astype(jnp.int32)


def level_of(stream_key, dims, cuts, least, top_value):
    def one(position, shards_of):
        draws = jax.random.uniform(jax.random.fold_in(jax.random.fold_in(stream_key, 6), position), (shards_of,), jnp.float32, least / len(cuts), top_value / len(cuts))
        return jnp.repeat(jnp.exp(draws), dims[position] // shards_of).reshape((-1,) + (1,) * (len(dims) - position - 1))

    loudness = one(*cuts[0])
    for cut in cuts[1:]:
        loudness = loudness * one(*cut)
    return loudness


def normal_values(stream_key, shape, spread, reach, shards=(), held_as=jnp.bfloat16):
    result = spread * jax.random.normal(stream_key, shape, jnp.float32)
    if shards:
        result = result * level_of(stream_key, shape, shards, -0.22, 0.18)
    return jnp.clip(result, -reach, reach).astype(held_as)


def setup_inputs(seed: int = 0, part: int = 0) -> dict:
    key_of = jax.random.split(jax.random.key(seed), 9)
    part_keys = jax.random.split(jax.random.fold_in(key_of[8], part), 9)
    queries = draw_queries(jax.random.fold_in(jax.random.fold_in(key_of[8], part), 71), part)
    prefix_keys = draw_prefix_keys(jax.random.fold_in(jax.random.fold_in(key_of[8], part), 71), part)
    prefix_values = normal_values(part_keys[2], (PREFIX, KVH, HD), 1.0, 6.0, ((0, 16),))
    suffix_keys = normal_values(part_keys[3], (SAMPLES, SUF, KVH, HD), 1.2, 7.0, ((0, 16),))
    suffix_values = normal_values(part_keys[4], (SAMPLES, SUF, KVH, HD), 1.0, 6.0, ((0, 16),))
    suffix_lengths = draw_suffix_lengths(jax.random.fold_in(jax.random.fold_in(key_of[8], part), 71), part)
    new_keys = draw_new_keys(jax.random.fold_in(jax.random.fold_in(key_of[8], part), 71), part)
    new_values = normal_values(part_keys[7], (SAMPLES, STEPS, KVH, HD), 1.0, 6.0, ((0, 16),))
    return dict(queries=queries, prefix_keys=prefix_keys, prefix_values=prefix_values, suffix_keys=suffix_keys, suffix_values=suffix_values, suffix_lengths=suffix_lengths, new_keys=new_keys, new_values=new_values)


def reference(queries, prefix_keys, prefix_values, suffix_keys, suffix_values, suffix_lengths, new_keys, new_values):
    group_size = H // KVH
    factor = 1.0 / jnp.sqrt(jnp.float32(HD))
    piece_keys = prefix_keys.astype(jnp.float32).reshape(N_SAMPLE, PRE_DEV, KVH, HD)
    piece_values = prefix_values.astype(jnp.float32).reshape(N_SAMPLE, PRE_DEV, KVH, HD)
    step_index = jnp.arange(STEPS, dtype=jnp.int32)
    causal = step_index[None, :] <= step_index[:, None]
    positions = jnp.arange(SUF, dtype=jnp.int32)

    def one_sample(sample_data):
        own_queries, own_keys, own_values, length, fresh_keys, fresh_values = sample_data
        query_rows = own_queries.astype(jnp.float32).reshape(STEPS, KVH, group_size, HD)
        scores = jnp.einsum('thgd,nphd->nthgp', query_rows, piece_keys, precision=lax.Precision.HIGHEST) * factor
        maxima = lax.optimization_barrier(jnp.max(scores, axis=-1))
        powers = jnp.exp(scores - maxima[..., None])
        totals = lax.optimization_barrier(jnp.sum(powers, axis=-1))
        sums = jnp.einsum('nthgp,nphd->nthgd', powers, piece_values, precision=lax.Precision.HIGHEST)
        pieces = sums / totals[..., None]
        log_totals = maxima + jnp.log(totals)
        all_keys = jnp.concatenate([own_keys, fresh_keys], axis=0).astype(jnp.float32)
        all_values = jnp.concatenate([own_values, fresh_values], axis=0).astype(jnp.float32)
        own_scores = jnp.einsum('thgd,phd->thgp', query_rows, all_keys, precision=lax.Precision.HIGHEST) * factor
        in_range = jnp.broadcast_to((positions < length)[None, :], (STEPS, SUF))
        usable = jnp.concatenate([in_range, causal], axis=1)[:, None, None, :]
        own_scores = jnp.where(usable, own_scores, -jnp.inf)
        own_max = lax.optimization_barrier(jnp.max(own_scores, axis=-1))
        own_powers = jnp.where(usable, jnp.exp(own_scores - own_max[..., None]), 0.0)
        own_total = lax.optimization_barrier(jnp.sum(own_powers, axis=-1))
        own_rounded = lax.optimization_barrier(own_powers.astype(jnp.bfloat16)).astype(jnp.float32)
        own_sum = jnp.einsum('thgp,phd->thgd', own_rounded, all_values, precision=lax.Precision.HIGHEST)
        highest = jnp.maximum(lax.optimization_barrier(jnp.max(log_totals, axis=0)), own_max)
        weights = jnp.exp(log_totals - highest[None])
        own_weight = jnp.exp(own_max - highest)
        upper = lax.optimization_barrier(jnp.sum(weights[..., None] * pieces, axis=0)) + own_weight[..., None] * own_sum
        lower = lax.optimization_barrier(jnp.sum(weights, axis=0)) + own_weight * own_total
        return (upper / lower[..., None]).reshape(STEPS, H, HD)
    return lax.map(one_sample, (queries, suffix_keys, suffix_values, suffix_lengths, new_keys, new_values))
```

```python
import functools
import math

import jax
import jax.numpy as jnp
from jax import lax
from jax.experimental import pallas as pl
from jax.experimental.pallas import tpu as pltpu
from jax.sharding import PartitionSpec as P

F32, BF16, I16 = jnp.float32, jnp.bfloat16, jnp.int16
STEPS_OF_CODE = 32767.0


def rows_of(tiles):
    wide = tiles.astype(F32)
    return wide.reshape(math.prod(wide.shape[:-1]), wide.shape[-1])


def nt_dot(a, b):
    return lax.dot_general(a, b, (((1,), (1,)), ((), ())), preferred_element_type=F32)


def kernel(
    n, group, chunk,
    lens, q_hbm, pk_hbm, pv_hbm, sk_hbm, sv_hbm, nk_hbm, nv_hbm,
    out_ref,
    q_own, pk, pv, wide, k_send, v_send, q_all, k_all, v_all, sk, sv, nk, nv, s_own,
    o_send, l_send, o_all, l_all, w_high, w_low, log_all, total_all,
    local_sem, suf_sem, block_sem, q_ss, q_rs, k_ss, k_rs, v_ss, v_rs, o_ss, o_rs, l_ss, l_rs,
):
    steps, kvh, gsize, dim = q_hbm.shape
    per = steps * gsize
    tokens = pk.shape[0] // kvh
    factor = 1.0 / math.sqrt(dim)
    me = lax.axis_index("sample")
    head = lax.rem(me, kvh)
    mine = lax.div(me, kvh)
    base = me - head
    chunks = sk.shape[0] // chunk
    blocks = n // kvh

    def remote(src, dst, ss, rs, dev):
        return pltpu.make_async_remote_copy(
            src_ref=src, dst_ref=dst, send_sem=ss, recv_sem=rs,
            device_id={"sample": dev}, device_id_type=pl.DeviceIdType.MESH,
        )

    def signal(sem, dev):
        pl.semaphore_signal(
            sem, inc=1, device_id={"sample": dev}, device_id_type=pl.DeviceIdType.MESH
        )

    def repeat(first, last, action):
        def body(d, _):
            action(d)
            return 0
        lax.fori_loop(first, last, body, 0)

    barrier = pltpu.get_barrier_semaphore()
    paired = blocks == 2
    second = base > 0
    other = lax.rem(base + kvh, n)
    if paired:
        repeat(1, kvh, lambda d: signal(barrier, base + lax.rem(head + d, kvh)))

        @pl.when(jnp.logical_not(second))
        def _():
            repeat(0, kvh, lambda d: signal(barrier, other + lax.rem(head + d, kvh)))
    else:
        repeat(1, n, lambda d: signal(barrier, lax.rem(me + d, n)))

    local = [
        pltpu.make_async_copy(a, b, local_sem.at[i])
        for i, (a, b) in enumerate(
            [(pk_hbm, pk), (pv_hbm, pv), (q_hbm, q_own), (nk_hbm, nk), (nv_hbm, nv)]
        )
    ]
    for c in local:
        c.start()
    own_q = pltpu.make_async_copy(q_hbm.at[:, head], q_all.at[me], q_rs.at[mine])
    own_q.start()
    halves = []
    for i, (a, b) in enumerate([(sk_hbm, sk), (sv_hbm, sv)]):
        for c in range(chunks):
            part = pl.ds(c * chunk, chunk)
            halves.append(
                pltpu.make_async_copy(a.at[part], b.at[part], suf_sem.at[i * chunks + c])
            )
    for c in halves:
        c.start()

    def split(src, copy, dst, kept):
        copy.wait()
        wide[...] = src[...].astype(F32)
        for h in range(kvh):
            dst[h] = wide[pl.ds(h, tokens, stride=kvh), :].astype(BF16)
        kept[head] = wide[pl.ds(head, tokens, stride=kvh), :].astype(BF16)

    def send_q(dev):
        remote(q_hbm.at[:, lax.rem(dev, kvh)], q_all.at[me], q_ss, q_rs.at[mine], dev).start()

    def send_kv(d, src, dst, ss, rs):
        hd = lax.rem(head + d, kvh)
        remote(src.at[hd], dst.at[head], ss, rs, base + hd).start()

    def near_q(d):
        send_q(base + lax.rem(head + d, kvh))

    def far_q(d):
        send_q(lax.rem(base + kvh + lax.rem(head + d, kvh) + lax.div(d, kvh) * kvh, n))

    def all_far_q():
        repeat(0, n - kvh, far_q)

    if paired:
        @pl.when(second)
        def _():
            pl.semaphore_wait(barrier, n - 1)
            repeat(0, kvh, lambda d: signal(block_sem, other + lax.rem(head + d, kvh)))
            all_far_q()

        @pl.when(jnp.logical_not(second))
        def _():
            pl.semaphore_wait(barrier, kvh - 1)
    else:
        pl.semaphore_wait(barrier, n - 1)
        all_far_q()
    repeat(1, kvh, near_q)
    split(pk, local[0], k_send, k_all)
    repeat(1, kvh, lambda d: send_kv(d, k_send, k_all, k_ss, k_rs))
    split(pv, local[1], v_send, v_all)
    if paired:
        @pl.when(jnp.logical_not(second))
        def _():
            pl.semaphore_wait(block_sem, kvh)
            all_far_q()
    repeat(1, kvh, lambda d: send_kv(d, v_send, v_all, v_ss, v_rs))

    for c in local[2:]:
        c.wait()
    rows = kvh * per
    q_rows = jnp.concatenate(
        [q_own[t, h].astype(F32) for h in range(kvh) for t in range(steps)], axis=0
    ).astype(BF16)
    length = lens[0]
    row = lax.broadcasted_iota(jnp.int32, (rows, 128), 0)
    lane = lax.broadcasted_iota(jnp.int32, (rows, 128), 1)
    lane_head = lax.rem(lane, kvh)
    match = (row >= lane_head * per) & (row < (lane_head + 1) * per)
    bias = jnp.where(match, 0.0, -jnp.inf).astype(F32)
    bias_wide = jnp.concatenate([bias] * (chunk // 128), axis=1)
    token_of = lax.div(lax.broadcasted_iota(jnp.int32, (8, chunk), 1), kvh)

    top = jnp.full((rows, 1), -jnp.inf, F32)
    for c in range(chunks):
        halves[c].wait()
        s = nt_dot(q_rows, sk[c * chunk:(c + 1) * chunk, :]) * factor
        limit = jnp.where(token_of < length - c * (chunk // kvh), 0.0, -jnp.inf).astype(F32)[:1]
        s = s + bias_wide + limit
        s_own[c] = s
        top = jnp.maximum(top, jnp.max(s, axis=-1, keepdims=True))

    pad = jnp.zeros((128 - steps * kvh, dim), F32)
    new_k = jnp.concatenate([nk[j].astype(F32) for j in range(steps)] + [pad], axis=0).astype(BF16)
    new_v = jnp.concatenate([nv[j].astype(F32) for j in range(steps)] + [pad], axis=0).astype(BF16)
    step_of = lax.div(lax.rem(row, per), gsize)
    s_new = nt_dot(q_rows, new_k) * factor + bias
    s_new = jnp.where(lax.div(lane, kvh) <= step_of, s_new, -jnp.inf)
    own_max = jnp.maximum(top, jnp.max(s_new, axis=-1, keepdims=True))
    w_new = jnp.exp(s_new - own_max)
    own_total = jnp.sum(w_new, axis=-1, keepdims=True)
    own_sum = jnp.dot(w_new.astype(BF16), new_v, preferred_element_type=F32)
    for c in range(chunks):
        halves[chunks + c].wait()
        w = jnp.exp(s_own[c] - own_max)
        own_total = own_total + jnp.sum(w, axis=-1, keepdims=True)
        own_sum = own_sum + jnp.dot(
            w.astype(BF16), sv[c * chunk:(c + 1) * chunk, :], preferred_element_type=F32
        )

    def settle(ref, sem):
        pltpu.make_async_copy(ref, ref, sem).wait()

    def others(ref):
        return ref.at[pl.ds(0, kvh - 1)]

    settle(others(k_all), k_rs)
    keys = k_all[...].reshape(kvh * tokens, dim)
    groups = kvh // group
    span = group * per

    def place(block, i):
        first = block * kvh + i * group
        return first, pl.ds(pl.multiple_of(first * per, span), span)

    def weigh(block):
        settle(q_all.at[pl.ds(block * kvh, kvh)], q_rs.at[block])

        def body(i):
            first, at = place(block, i)
            q_block = rows_of(q_all[pl.ds(first, group)]).astype(BF16)
            s = nt_dot(q_block, keys) * factor
            m = jnp.max(s, axis=-1, keepdims=True)
            w = jnp.exp(s - m)
            total = jnp.sum(w, axis=-1, keepdims=True)
            high = w.astype(BF16)
            w_high[at] = high
            w_low[at] = (w - high.astype(F32)).astype(BF16)
            total_all[at] = total
            log_all[at] = m + jnp.log(total)

        repeat(0, groups, body)

    repeat(0, blocks, lambda b: weigh(lax.rem(mine + b, blocks)))

    settle(others(v_all), v_rs)
    values = v_all[...].reshape(kvh * tokens, dim)
    diag_row = lax.broadcasted_iota(jnp.int32, (per, 128), 0)
    diag_lane = lax.broadcasted_iota(jnp.int32, (per, 128), 1)
    at_log = diag_lane == diag_row
    at_unit = diag_lane == diag_row + 64

    def emit(block):
        def body(i):
            first, at = place(block, i)
            sums = jnp.dot(w_high[at], values, preferred_element_type=F32) + jnp.dot(
                w_low[at], values, preferred_element_type=F32
            )
            largest = jnp.maximum(jnp.max(jnp.abs(sums), axis=-1, keepdims=True), 1e-30)
            code = jnp.round(sums * (STEPS_OF_CODE / largest)).astype(jnp.int32).astype(I16)
            o_send[pl.ds(first, group)] = code.reshape(group, steps, gsize, dim)
            unit = largest / (STEPS_OF_CODE * total_all[at])
            both = jnp.where(
                at_log[None],
                jnp.broadcast_to(log_all[at], (span, 128)).reshape(group, per, 128),
                jnp.where(
                    at_unit[None],
                    jnp.broadcast_to(unit, (span, 128)).reshape(group, per, 128),
                    0.0,
                ),
            )
            l_send[pl.ds(first, group)] = jnp.sum(both, axis=1, keepdims=True)
            for j in range(group):
                dev = first + j

                @pl.when(dev != me)
                def _():
                    remote(o_send.at[dev], o_all.at[me], o_ss, o_rs.at[mine], dev).start()
                    remote(l_send.at[dev], l_all.at[me], l_ss, l_rs.at[mine], dev).start()

                @pl.when(dev == me)
                def _():
                    pltpu.make_async_copy(o_send.at[dev], o_all.at[dev], o_rs.at[mine]).start()
                    pltpu.make_async_copy(l_send.at[dev], l_all.at[dev], l_rs.at[mine]).start()

        repeat(0, groups, body)

    repeat(1, blocks + 1, lambda b: emit(lax.rem(mine + b, blocks)))

    highest, upper, lower = own_max, own_sum, own_total
    for r in range(blocks):
        part = pl.ds(r * kvh, kvh)
        settle(l_all.at[part], l_rs.at[r])
        spread = jnp.broadcast_to(l_all[part], (kvh, per, 128))

        def column(where):
            return jnp.sum(
                jnp.where(where[None], spread, 0.0), axis=-1, keepdims=True
            ).reshape(rows, 1)

        log = column(at_log)
        unit = column(at_unit)
        now = jnp.maximum(highest, log)
        keep, weight = jnp.exp(highest - now), jnp.exp(log - now)
        settle(o_all.at[part], o_rs.at[r])
        piece = o_all[part].astype(jnp.int32).astype(F32).reshape(rows, dim)
        upper = upper * keep + (weight * unit) * piece
        lower = lower * keep + weight
        highest = now
    result = upper / lower
    for h in range(kvh):
        for t in range(steps):
            at = h * per + t * gsize
            out_ref[t, h] = result[at:at + gsize]

    settle(q_all.at[pl.ds(0, n - 1)], q_ss)
    settle(others(k_all), k_ss)
    settle(others(v_all), v_ss)
    settle(o_all.at[pl.ds(0, n - 1)], o_ss)
    settle(l_all.at[pl.ds(0, n - 1)], l_ss)


def solution(mesh):
    n = mesh.shape["sample"]

    def shards(queries, pk, pv, sk, sv, lengths, nk, nv):
        _, steps, heads, dim = queries.shape
        tokens, kvh, _ = pk.shape
        gsize = heads // kvh
        suffix = sk.shape[1]
        per = steps * gsize
        group = math.gcd(kvh, 4)
        chunk = math.gcd(suffix * kvh, 1024)
        chunks = suffix * kvh // chunk
        dma = pltpu.SemaphoreType.DMA
        out = pl.pallas_call(
            functools.partial(kernel, n, group, chunk),
            out_shape=jax.ShapeDtypeStruct((steps, kvh, gsize, dim), F32),
            in_specs=[pl.BlockSpec(memory_space=pltpu.SMEM)]
            + [pl.BlockSpec(memory_space=pltpu.HBM)] * 7,
            out_specs=pl.BlockSpec(memory_space=pltpu.VMEM),
            scratch_shapes=[
                pltpu.VMEM((steps, kvh, gsize, dim), BF16),
                pltpu.VMEM((tokens * kvh, dim), BF16),
                pltpu.VMEM((tokens * kvh, dim), BF16),
                pltpu.VMEM((tokens * kvh, dim), F32),
                pltpu.VMEM((kvh, tokens, dim), BF16),
                pltpu.VMEM((kvh, tokens, dim), BF16),
                pltpu.VMEM((n, steps, gsize, dim), BF16),
                pltpu.VMEM((kvh, tokens, dim), BF16),
                pltpu.VMEM((kvh, tokens, dim), BF16),
                pltpu.VMEM((suffix * kvh, dim), BF16),
                pltpu.VMEM((suffix * kvh, dim), BF16),
                pltpu.VMEM((steps, kvh, dim), BF16),
                pltpu.VMEM((steps, kvh, dim), BF16),
                pltpu.VMEM((chunks, kvh * per, chunk), F32),
                pltpu.VMEM((n, steps, gsize, dim), I16),
                pltpu.VMEM((n, 1, 128), F32),
                pltpu.VMEM((n, steps, gsize, dim), I16),
                pltpu.VMEM((n, 1, 128), F32),
                pltpu.VMEM((n * per, kvh * tokens), BF16),
                pltpu.VMEM((n * per, kvh * tokens), BF16),
                pltpu.VMEM((n * per, 1), F32),
                pltpu.VMEM((n * per, 1), F32),
                dma((5,)), dma((2 * chunks,)), pltpu.SemaphoreType.REGULAR,
                dma, dma((n // kvh,)), dma, dma, dma, dma,
                dma, dma((n // kvh,)), dma, dma((n // kvh,)),
            ],
            compiler_params=pltpu.CompilerParams(
                collective_id=0, has_side_effects=True, vmem_limit_bytes=48 << 20
            ),
        )(lengths, *[pltpu.with_memory_space_constraint(x, pltpu.HBM) for x in (
            queries.reshape(steps, kvh, gsize, dim),
            pk.reshape(tokens * kvh, dim),
            pv.reshape(tokens * kvh, dim),
            sk.reshape(suffix * kvh, dim),
            sv.reshape(suffix * kvh, dim),
            nk.reshape(steps, kvh, dim),
            nv.reshape(steps, kvh, dim),
        )])
        return out.reshape(1, steps, heads, dim)

    spread = ("group", "sample")
    four = P(spread, None, None, None)
    three = P(spread, None, None)
    return jax.shard_map(
        shards, mesh=mesh,
        in_specs=(four, three, three, four, four, P(spread), four, four),
        out_specs=four, check_vma=False,
    )
```

```python
import functools
import math

import jax
import jax.numpy as jnp
from jax import lax
from jax.experimental import pallas as pl
from jax.experimental.pallas import tpu as pltpu
from jax.sharding import PartitionSpec as P

F32, BF16, I16 = jnp.float32, jnp.bfloat16, jnp.int16
STEPS_OF_CODE = 32767.0


def rows_of(tiles):
    wide = tiles.astype(F32)
    return wide.reshape(math.prod(wide.shape[:-1]), wide.shape[-1])


def nt_dot(a, b):
    return lax.dot_general(a, b, (((1,), (1,)), ((), ())), preferred_element_type=F32)


def kernel(
    n, group, chunk,
    lens, q_hbm, pk_hbm, pv_hbm, sk_hbm, sv_hbm, nk_hbm, nv_hbm,
    out_ref,
    q_own, pk, pv, wide, k_send, v_send, q_all, k_all, v_all, sk, sv, nk, nv, s_own,
    o_send, l_send, o_all, l_all, w_high, w_low, log_all, total_all,
    local_sem, suf_sem, late_sem, block_sem, q_ss, q_rs, k_ss, k_rs, v_ss, v_rs, o_ss, o_rs, l_ss, l_rs,
):
    steps, kvh, gsize, dim = q_hbm.shape
    per = steps * gsize
    tokens = pk.shape[0] // kvh
    factor = 1.0 / math.sqrt(dim)
    me = lax.axis_index("sample")
    head = lax.rem(me, kvh)
    mine = lax.div(me, kvh)
    base = me - head
    chunks = sk.shape[0] // chunk
    blocks = n // kvh

    def remote(src, dst, ss, rs, dev):
        return pltpu.make_async_remote_copy(
            src_ref=src, dst_ref=dst, send_sem=ss, recv_sem=rs,
            device_id={"sample": dev}, device_id_type=pl.DeviceIdType.MESH,
        )

    def signal(sem, dev):
        pl.semaphore_signal(
            sem, inc=1, device_id={"sample": dev}, device_id_type=pl.DeviceIdType.MESH
        )

    def repeat(first, last, action):
        def body(d, _):
            action(d)
            return 0
        lax.fori_loop(first, last, body, 0)

    local = [
        pltpu.make_async_copy(a, b, local_sem.at[i])
        for i, (a, b) in enumerate(
            [(pk_hbm, pk), (pv_hbm, pv), (q_hbm, q_own), (nk_hbm, nk), (nv_hbm, nv)]
        )
    ]
    local[0].start()

    barrier = pltpu.get_barrier_semaphore()
    paired = blocks == 2 and kvh % 2 == 0 and kvh >= 4
    second = base > 0
    other = lax.rem(base + kvh, n)
    early = kvh - 2 if paired else kvh
    late = head >= early

    def to_early(action):
        repeat(jnp.where(late, 0, 1), early, lambda d: action(lax.rem(head + d, early)))

    def to_late(action):
        if paired:
            repeat(
                0, jnp.where(late, 1, 2), lambda d: action(early + lax.rem(head + 1 + d, 2))
            )

    def unless(skipped, action):
        pl.when(jnp.logical_not(skipped))(action)

    if paired:
        unless(late, lambda: to_early(lambda hd: signal(barrier, base + hd)))
        to_late(lambda hd: signal(barrier, base + hd))
        unless(second, lambda: repeat(early, kvh, lambda hd: signal(barrier, other + hd)))
    else:
        repeat(1, n, lambda d: signal(barrier, lax.rem(me + d, n)))

    for c in local[1:]:
        c.start()
    own_q = pltpu.make_async_copy(q_hbm.at[:, head], q_all.at[me], q_rs.at[mine])
    own_q.start()
    halves = []
    for i, (a, b) in enumerate([(sk_hbm, sk), (sv_hbm, sv)]):
        for c in range(chunks):
            part = pl.ds(c * chunk, chunk)
            halves.append(
                pltpu.make_async_copy(a.at[part], b.at[part], suf_sem.at[i * chunks + c])
            )
    for c in halves:
        c.start()

    def split(src, copy, dst, kept):
        copy.wait()
        wide[...] = src[...].astype(F32)
        for h in range(kvh):
            dst[h] = wide[pl.ds(h, tokens, stride=kvh), :].astype(BF16)
        kept[head] = wide[pl.ds(head, tokens, stride=kvh), :].astype(BF16)

    def send_q(dev):
        remote(q_hbm.at[:, lax.rem(dev, kvh)], q_all.at[me], q_ss, q_rs.at[mine], dev).start()

    def send_k(hd):
        remote(k_send.at[hd], k_all.at[head], k_ss, k_rs, base + hd).start()

    def send_v(hd):
        remote(v_send.at[hd], v_all.at[head], v_ss, v_rs, base + hd).start()

    def near_q(hd):
        send_q(base + hd)

    def far_q():
        repeat(0, n - kvh, lambda d: send_q(
            lax.rem(base + kvh + lax.rem(head + d, kvh) + lax.div(d, kvh) * kvh, n)
        ))

    if paired:
        @pl.when(late)
        def _():
            pl.semaphore_wait(barrier, jnp.where(second, n - 1, kvh - 1))
            repeat(0, early, lambda hd: signal(late_sem, base + hd))

            @pl.when(second)
            def _():
                repeat(0, kvh // 2, lambda d: signal(block_sem, other + 2 * d + head - early))

        unless(late, lambda: pl.semaphore_wait(barrier, early - 1))
    else:
        pl.semaphore_wait(barrier, n - 1)
    to_early(near_q)
    split(pk, local[0], k_send, k_all)
    to_early(send_k)
    if paired:
        unless(late, lambda: pl.semaphore_wait(late_sem, 2))
        to_late(near_q)
        to_late(send_k)
        pl.when(second)(far_q)
    else:
        far_q()
    split(pv, local[1], v_send, v_all)
    if paired:
        @pl.when(jnp.logical_not(second))
        def _():
            pl.semaphore_wait(block_sem, 1)
            far_q()
    to_early(send_v)
    to_late(send_v)

    for c in local[2:]:
        c.wait()
    rows = kvh * per
    q_rows = jnp.concatenate(
        [q_own[t, h].astype(F32) for h in range(kvh) for t in range(steps)], axis=0
    ).astype(BF16)
    length = lens[0]
    row = lax.broadcasted_iota(jnp.int32, (rows, 128), 0)
    lane = lax.broadcasted_iota(jnp.int32, (rows, 128), 1)
    lane_head = lax.rem(lane, kvh)
    match = (row >= lane_head * per) & (row < (lane_head + 1) * per)
    bias = jnp.where(match, 0.0, -jnp.inf).astype(F32)
    bias_wide = jnp.concatenate([bias] * (chunk // 128), axis=1)
    token_of = lax.div(lax.broadcasted_iota(jnp.int32, (8, chunk), 1), kvh)

    top = jnp.full((rows, 1), -jnp.inf, F32)
    for c in range(chunks):
        halves[c].wait()
        s = nt_dot(q_rows, sk[c * chunk:(c + 1) * chunk, :]) * factor
        limit = jnp.where(token_of < length - c * (chunk // kvh), 0.0, -jnp.inf).astype(F32)[:1]
        s = s + bias_wide + limit
        s_own[c] = s
        top = jnp.maximum(top, jnp.max(s, axis=-1, keepdims=True))

    pad = jnp.zeros((128 - steps * kvh, dim), F32)
    new_k = jnp.concatenate([nk[j].astype(F32) for j in range(steps)] + [pad], axis=0).astype(BF16)
    new_v = jnp.concatenate([nv[j].astype(F32) for j in range(steps)] + [pad], axis=0).astype(BF16)
    step_of = lax.div(lax.rem(row, per), gsize)
    s_new = nt_dot(q_rows, new_k) * factor + bias
    s_new = jnp.where(lax.div(lane, kvh) <= step_of, s_new, -jnp.inf)
    own_max = jnp.maximum(top, jnp.max(s_new, axis=-1, keepdims=True))
    w_new = jnp.exp(s_new - own_max)
    own_total = jnp.sum(w_new, axis=-1, keepdims=True)
    own_sum = jnp.dot(w_new.astype(BF16), new_v, preferred_element_type=F32)
    for c in range(chunks):
        halves[chunks + c].wait()
        w = jnp.exp(s_own[c] - own_max)
        own_total = own_total + jnp.sum(w, axis=-1, keepdims=True)
        own_sum = own_sum + jnp.dot(
            w.astype(BF16), sv[c * chunk:(c + 1) * chunk, :], preferred_element_type=F32
        )

    def settle(ref, sem):
        pltpu.make_async_copy(ref, ref, sem).wait()

    def others(ref):
        return ref.at[pl.ds(0, kvh - 1)]

    settle(others(k_all), k_rs)
    keys = k_all[...].reshape(kvh * tokens, dim)
    groups = kvh // group
    span = group * per

    def place(block, i):
        first = block * kvh + i * group
        return first, pl.ds(pl.multiple_of(first * per, span), span)

    def weigh(block):
        settle(q_all.at[pl.ds(block * kvh, kvh)], q_rs.at[block])

        def body(i):
            first, at = place(block, i)
            q_block = rows_of(q_all[pl.ds(first, group)]).astype(BF16)
            s = nt_dot(q_block, keys) * factor
            m = jnp.max(s, axis=-1, keepdims=True)
            w = jnp.exp(s - m)
            total = jnp.sum(w, axis=-1, keepdims=True)
            high = w.astype(BF16)
            w_high[at] = high
            w_low[at] = (w - high.astype(F32)).astype(BF16)
            total_all[at] = total
            log_all[at] = m + jnp.log(total)

        repeat(0, groups, body)

    repeat(0, blocks, lambda b: weigh(lax.rem(mine + b, blocks)))

    settle(others(v_all), v_rs)
    values = v_all[...].reshape(kvh * tokens, dim)
    diag_row = lax.broadcasted_iota(jnp.int32, (per, 128), 0)
    diag_lane = lax.broadcasted_iota(jnp.int32, (per, 128), 1)
    at_log = diag_lane == diag_row
    at_unit = diag_lane == diag_row + 64

    def emit(block):
        def body(i):
            first, at = place(block, i)
            sums = jnp.dot(w_high[at], values, preferred_element_type=F32) + jnp.dot(
                w_low[at], values, preferred_element_type=F32
            )
            largest = jnp.maximum(jnp.max(jnp.abs(sums), axis=-1, keepdims=True), 1e-30)
            code = jnp.round(sums * (STEPS_OF_CODE / largest)).astype(jnp.int32).astype(I16)
            o_send[pl.ds(first, group)] = code.reshape(group, steps, gsize, dim)
            unit = largest / (STEPS_OF_CODE * total_all[at])
            both = jnp.where(
                at_log[None],
                jnp.broadcast_to(log_all[at], (span, 128)).reshape(group, per, 128),
                jnp.where(
                    at_unit[None],
                    jnp.broadcast_to(unit, (span, 128)).reshape(group, per, 128),
                    0.0,
                ),
            )
            l_send[pl.ds(first, group)] = jnp.sum(both, axis=1, keepdims=True)
            for j in range(group):
                dev = first + j

                @pl.when(dev != me)
                def _():
                    remote(o_send.at[dev], o_all.at[me], o_ss, o_rs.at[mine], dev).start()
                    remote(l_send.at[dev], l_all.at[me], l_ss, l_rs.at[mine], dev).start()

                @pl.when(dev == me)
                def _():
                    pltpu.make_async_copy(o_send.at[dev], o_all.at[dev], o_rs.at[mine]).start()
                    pltpu.make_async_copy(l_send.at[dev], l_all.at[dev], l_rs.at[mine]).start()

        repeat(0, groups, body)

    repeat(1, blocks + 1, lambda b: emit(lax.rem(mine + b, blocks)))

    highest, upper, lower = own_max, own_sum, own_total
    for r in range(blocks):
        part = pl.ds(r * kvh, kvh)
        settle(l_all.at[part], l_rs.at[r])
        spread = jnp.broadcast_to(l_all[part], (kvh, per, 128))

        def column(where):
            return jnp.sum(
                jnp.where(where[None], spread, 0.0), axis=-1, keepdims=True
            ).reshape(rows, 1)

        log = column(at_log)
        unit = column(at_unit)
        now = jnp.maximum(highest, log)
        keep, weight = jnp.exp(highest - now), jnp.exp(log - now)
        settle(o_all.at[part], o_rs.at[r])
        piece = o_all[part].astype(jnp.int32).astype(F32).reshape(rows, dim)
        upper = upper * keep + (weight * unit) * piece
        lower = lower * keep + weight
        highest = now
    result = upper / lower
    for h in range(kvh):
        for t in range(steps):
            at = h * per + t * gsize
            out_ref[t, h] = result[at:at + gsize]

    settle(q_all.at[pl.ds(0, n - 1)], q_ss)
    settle(others(k_all), k_ss)
    settle(others(v_all), v_ss)
    settle(o_all.at[pl.ds(0, n - 1)], o_ss)
    settle(l_all.at[pl.ds(0, n - 1)], l_ss)


def solution(mesh):
    n = mesh.shape["sample"]

    def shards(queries, pk, pv, sk, sv, lengths, nk, nv):
        _, steps, heads, dim = queries.shape
        tokens, kvh, _ = pk.shape
        gsize = heads // kvh
        suffix = sk.shape[1]
        per = steps * gsize
        group = math.gcd(kvh, 4)
        chunk = math.gcd(suffix * kvh, 1024)
        chunks = suffix * kvh // chunk
        dma = pltpu.SemaphoreType.DMA
        out = pl.pallas_call(
            functools.partial(kernel, n, group, chunk),
            out_shape=jax.ShapeDtypeStruct((steps, kvh, gsize, dim), F32),
            in_specs=[pl.BlockSpec(memory_space=pltpu.SMEM)]
            + [pl.BlockSpec(memory_space=pltpu.HBM)] * 7,
            out_specs=pl.BlockSpec(memory_space=pltpu.VMEM),
            scratch_shapes=[
                pltpu.VMEM((steps, kvh, gsize, dim), BF16),
                pltpu.VMEM((tokens * kvh, dim), BF16),
                pltpu.VMEM((tokens * kvh, dim), BF16),
                pltpu.VMEM((tokens * kvh, dim), F32),
                pltpu.VMEM((kvh, tokens, dim), BF16),
                pltpu.VMEM((kvh, tokens, dim), BF16),
                pltpu.VMEM((n, steps, gsize, dim), BF16),
                pltpu.VMEM((kvh, tokens, dim), BF16),
                pltpu.VMEM((kvh, tokens, dim), BF16),
                pltpu.VMEM((suffix * kvh, dim), BF16),
                pltpu.VMEM((suffix * kvh, dim), BF16),
                pltpu.VMEM((steps, kvh, dim), BF16),
                pltpu.VMEM((steps, kvh, dim), BF16),
                pltpu.VMEM((chunks, kvh * per, chunk), F32),
                pltpu.VMEM((n, steps, gsize, dim), I16),
                pltpu.VMEM((n, 1, 128), F32),
                pltpu.VMEM((n, steps, gsize, dim), I16),
                pltpu.VMEM((n, 1, 128), F32),
                pltpu.VMEM((n * per, kvh * tokens), BF16),
                pltpu.VMEM((n * per, kvh * tokens), BF16),
                pltpu.VMEM((n * per, 1), F32),
                pltpu.VMEM((n * per, 1), F32),
                dma((5,)), dma((2 * chunks,)),
                pltpu.SemaphoreType.REGULAR, pltpu.SemaphoreType.REGULAR,
                dma, dma((n // kvh,)), dma, dma, dma, dma,
                dma, dma((n // kvh,)), dma, dma((n // kvh,)),
            ],
            compiler_params=pltpu.CompilerParams(
                collective_id=0, has_side_effects=True, vmem_limit_bytes=48 << 20
            ),
        )(lengths, *[pltpu.with_memory_space_constraint(x, pltpu.HBM) for x in (
            queries.reshape(steps, kvh, gsize, dim),
            pk.reshape(tokens * kvh, dim),
            pv.reshape(tokens * kvh, dim),
            sk.reshape(suffix * kvh, dim),
            sv.reshape(suffix * kvh, dim),
            nk.reshape(steps, kvh, dim),
            nv.reshape(steps, kvh, dim),
        )])
        return out.reshape(1, steps, heads, dim)

    spread = ("group", "sample")
    four = P(spread, None, None, None)
    three = P(spread, None, None)
    return jax.shard_map(
        shards, mesh=mesh,
        in_specs=(four, three, three, four, four, P(spread), four, four),
        out_specs=four, check_vma=False,
    )
```

```python
import functools
import math

import jax
import jax.numpy as jnp
from jax import lax
from jax.experimental import pallas as pl
from jax.experimental.pallas import tpu as pltpu
from jax.sharding import PartitionSpec as P

F32, BF16, I16 = jnp.float32, jnp.bfloat16, jnp.int16
CODES = 32767.0
PARTS = 65535.0


def rows_of(tiles):
    wide = tiles.astype(F32)
    return wide.reshape(math.prod(wide.shape[:-1]), wide.shape[-1])


def nt_dot(a, b):
    return lax.dot_general(a, b, (((1,), (1,)), ((), ())), preferred_element_type=F32)


def kernel(
    n, group, chunk,
    lens, q_hbm, pk_hbm, pv_hbm, sk_hbm, sv_hbm, nk_hbm, nv_hbm,
    out_ref,
    q_own, pk, pv, wide, k_send, v_send, q_all, k_all, v_all, sk, sv, nk, nv, s_own,
    o_send, o_all, w_high, w_low, log_all, total_all,
    local_sem, suf_sem, late_sem, block_sem, q_ss, q_rs, k_ss, k_rs, v_ss, v_rs, o_ss, o_rs,
):
    steps, kvh, gsize, dim = q_hbm.shape
    per = steps * gsize
    tokens = pk.shape[0] // kvh
    factor = 1.0 / math.sqrt(dim)
    me = lax.axis_index("sample")
    head = lax.rem(me, kvh)
    mine = lax.div(me, kvh)
    base = me - head
    chunks = sk.shape[0] // chunk
    blocks = n // kvh

    def remote(src, dst, ss, rs, dev):
        return pltpu.make_async_remote_copy(
            src_ref=src, dst_ref=dst, send_sem=ss, recv_sem=rs,
            device_id={"sample": dev}, device_id_type=pl.DeviceIdType.MESH,
        )

    def signal(sem, dev):
        pl.semaphore_signal(
            sem, inc=1, device_id={"sample": dev}, device_id_type=pl.DeviceIdType.MESH
        )

    def repeat(first, last, action):
        def body(d, _):
            action(d)
            return 0
        lax.fori_loop(first, last, body, 0)

    local = [
        pltpu.make_async_copy(a, b, local_sem.at[i])
        for i, (a, b) in enumerate(
            [(pk_hbm, pk), (pv_hbm, pv), (q_hbm, q_own), (nk_hbm, nk), (nv_hbm, nv)]
        )
    ]
    local[0].start()

    barrier = pltpu.get_barrier_semaphore()
    paired = blocks == 2 and kvh % 2 == 0 and kvh >= 4
    second = base > 0
    other = lax.rem(base + kvh, n)
    early = kvh - 2 if paired else kvh
    late = head >= early

    def to_early(action):
        repeat(jnp.where(late, 0, 1), early, lambda d: action(lax.rem(head + d, early)))

    def to_late(action):
        if paired:
            repeat(
                0, jnp.where(late, 1, 2), lambda d: action(early + lax.rem(head + 1 + d, 2))
            )

    def unless(skipped, action):
        pl.when(jnp.logical_not(skipped))(action)

    if paired:
        unless(late, lambda: to_early(lambda hd: signal(barrier, base + hd)))
        to_late(lambda hd: signal(barrier, base + hd))
        unless(second, lambda: repeat(early, kvh, lambda hd: signal(barrier, other + hd)))
    else:
        repeat(1, n, lambda d: signal(barrier, lax.rem(me + d, n)))

    for c in local[1:]:
        c.start()
    own_q = pltpu.make_async_copy(q_hbm.at[:, head], q_all.at[me], q_rs.at[mine])
    own_q.start()
    halves = []
    for i, (a, b) in enumerate([(sk_hbm, sk), (sv_hbm, sv)]):
        for c in range(chunks):
            part = pl.ds(c * chunk, chunk)
            halves.append(
                pltpu.make_async_copy(a.at[part], b.at[part], suf_sem.at[i * chunks + c])
            )
    for c in halves:
        c.start()

    def split(src, copy, dst, kept):
        copy.wait()
        wide[...] = src[...].astype(F32)
        for h in range(kvh):
            dst[h] = wide[pl.ds(h, tokens, stride=kvh), :].astype(BF16)
        kept[head] = wide[pl.ds(head, tokens, stride=kvh), :].astype(BF16)

    def send_q(dev):
        remote(q_hbm.at[:, lax.rem(dev, kvh)], q_all.at[me], q_ss, q_rs.at[mine], dev).start()

    def send_k(hd):
        remote(k_send.at[hd], k_all.at[head], k_ss, k_rs, base + hd).start()

    def send_v(hd):
        remote(v_send.at[hd], v_all.at[head], v_ss, v_rs, base + hd).start()

    def near_q(hd):
        send_q(base + hd)

    def far_q():
        repeat(0, n - kvh, lambda d: send_q(
            lax.rem(base + kvh + lax.rem(head + d, kvh) + lax.div(d, kvh) * kvh, n)
        ))

    if paired:
        @pl.when(late)
        def _():
            pl.semaphore_wait(barrier, jnp.where(second, n - 1, kvh - 1))
            repeat(0, early, lambda hd: signal(late_sem, base + hd))

            @pl.when(second)
            def _():
                repeat(0, kvh // 2, lambda d: signal(block_sem, other + 2 * d + head - early))

        unless(late, lambda: pl.semaphore_wait(barrier, early - 1))
    else:
        pl.semaphore_wait(barrier, n - 1)
    to_early(near_q)
    split(pk, local[0], k_send, k_all)
    to_early(send_k)
    if paired:
        unless(late, lambda: pl.semaphore_wait(late_sem, 2))
        to_late(near_q)
        to_late(send_k)
        pl.when(second)(far_q)
    else:
        far_q()
    split(pv, local[1], v_send, v_all)
    if paired:
        @pl.when(jnp.logical_not(second))
        def _():
            pl.semaphore_wait(block_sem, 1)
            far_q()
    to_early(send_v)
    to_late(send_v)

    for c in local[2:]:
        c.wait()
    rows = kvh * per
    q_rows = jnp.concatenate(
        [q_own[t, h].astype(F32) for h in range(kvh) for t in range(steps)], axis=0
    ).astype(BF16)
    length = lens[0]
    row = lax.broadcasted_iota(jnp.int32, (rows, 128), 0)
    lane = lax.broadcasted_iota(jnp.int32, (rows, 128), 1)
    lane_head = lax.rem(lane, kvh)
    match = (row >= lane_head * per) & (row < (lane_head + 1) * per)
    bias = jnp.where(match, 0.0, -jnp.inf).astype(F32)
    bias_wide = jnp.concatenate([bias] * (chunk // 128), axis=1)
    token_of = lax.div(lax.broadcasted_iota(jnp.int32, (8, chunk), 1), kvh)

    top = jnp.full((rows, 1), -jnp.inf, F32)
    for c in range(chunks):
        halves[c].wait()
        s = nt_dot(q_rows, sk[c * chunk:(c + 1) * chunk, :]) * factor
        limit = jnp.where(token_of < length - c * (chunk // kvh), 0.0, -jnp.inf).astype(F32)[:1]
        s = s + bias_wide + limit
        s_own[c] = s
        top = jnp.maximum(top, jnp.max(s, axis=-1, keepdims=True))

    pad = jnp.zeros((128 - steps * kvh, dim), F32)
    new_k = jnp.concatenate([nk[j].astype(F32) for j in range(steps)] + [pad], axis=0).astype(BF16)
    new_v = jnp.concatenate([nv[j].astype(F32) for j in range(steps)] + [pad], axis=0).astype(BF16)
    step_of = lax.div(lax.rem(row, per), gsize)
    s_new = nt_dot(q_rows, new_k) * factor + bias
    s_new = jnp.where(lax.div(lane, kvh) <= step_of, s_new, -jnp.inf)
    own_max = jnp.maximum(top, jnp.max(s_new, axis=-1, keepdims=True))
    w_new = jnp.exp(s_new - own_max)
    own_total = jnp.sum(w_new, axis=-1, keepdims=True)
    own_sum = jnp.dot(w_new.astype(BF16), new_v, preferred_element_type=F32)
    for c in range(chunks):
        halves[chunks + c].wait()
        w = jnp.exp(s_own[c] - own_max)
        own_total = own_total + jnp.sum(w, axis=-1, keepdims=True)
        own_sum = own_sum + jnp.dot(
            w.astype(BF16), sv[c * chunk:(c + 1) * chunk, :], preferred_element_type=F32
        )

    def settle(ref, sem):
        pltpu.make_async_copy(ref, ref, sem).wait()

    def others(ref):
        return ref.at[pl.ds(0, kvh - 1)]

    settle(others(k_all), k_rs)
    keys = k_all[...].reshape(kvh * tokens, dim)
    groups = kvh // group
    span = group * per

    def place(block, i):
        first = block * kvh + i * group
        return first, pl.ds(pl.multiple_of(first * per, span), span)

    def weigh(block):
        settle(q_all.at[pl.ds(block * kvh, kvh)], q_rs.at[block])

        def body(i):
            first, at = place(block, i)
            q_block = rows_of(q_all[pl.ds(first, group)]).astype(BF16)
            s = nt_dot(q_block, keys)
            m = jnp.max(s, axis=-1, keepdims=True)
            w = jnp.exp2((s - m) * (factor * math.log2(math.e)))
            total = jnp.sum(w, axis=-1, keepdims=True)
            high = w.astype(BF16)
            w_high[at] = high
            w_low[at] = (w - high.astype(F32)).astype(BF16)
            total_all[at] = total
            log_all[at] = m * factor + jnp.log(total)

        repeat(0, groups, body)

    repeat(0, blocks, lambda b: weigh(lax.rem(mine + b, blocks)))

    settle(others(v_all), v_rs)
    values = v_all[...].reshape(kvh * tokens, dim)
    diag_row = lax.broadcasted_iota(jnp.int32, (per, 128), 0)
    diag_lane = lax.broadcasted_iota(jnp.int32, (per, 128), 1)
    at_whole = diag_lane == diag_row
    at_part = diag_lane == diag_row + 32
    at_power = diag_lane == diag_row + 64
    pairs = per // 2

    def emit(block):
        def body(i):
            first, at = place(block, i)
            sums = jnp.dot(w_high[at], values, preferred_element_type=F32) + jnp.dot(
                w_low[at], values, preferred_element_type=F32
            )
            total = total_all[at]
            largest = jnp.max(jnp.abs(sums), axis=-1, keepdims=True)
            power = jnp.ceil(jnp.log2(jnp.maximum(largest / total, 1e-30)))
            code = jnp.round(sums * (CODES * jnp.exp2(-power) / total))
            log = log_all[at]
            whole = jnp.floor(log)
            part = jnp.round((log - whole) * PARTS) - 32768.0

            def lanes(column):
                return jnp.broadcast_to(column, (span, 128)).reshape(group, per, 128)

            facts = jnp.where(at_whole[None], lanes(whole), jnp.where(
                at_part[None], lanes(part), jnp.where(at_power[None], lanes(power), 0.0)
            ))
            facts = jnp.broadcast_to(jnp.sum(facts, axis=1, keepdims=True), (group, 2, 128))
            here = pl.ds(first, group)
            o_send[here, 0:pairs] = code.astype(jnp.int32).astype(I16).reshape(group, pairs, 2, dim)
            o_send[here, pairs:] = facts.astype(jnp.int32).astype(I16).reshape(group, 1, 2, dim)
            for j in range(group):
                dev = first + j

                @pl.when(dev != me)
                def _():
                    remote(o_send.at[dev], o_all.at[me], o_ss, o_rs.at[mine], dev).start()

                @pl.when(dev == me)
                def _():
                    pltpu.make_async_copy(o_send.at[dev], o_all.at[dev], o_rs.at[mine]).start()

        repeat(0, groups, body)

    repeat(1, blocks + 1, lambda b: emit(lax.rem(mine + b, blocks)))

    log_scales = jnp.where(at_whole, 1.0, jnp.where(at_part, 1.0 / PARTS, 0.0))
    highest, upper, lower = own_max, own_sum, own_total
    for r in range(blocks):
        part = pl.ds(r * kvh, kvh)
        settle(o_all.at[part], o_rs.at[r])
        facts = o_all[part, pairs:].astype(jnp.int32).astype(F32)
        spread = jnp.broadcast_to(facts.reshape(kvh, 2, 128)[:, 0:1], (kvh, per, 128))

        def column(scales):
            return jnp.sum(spread * scales[None], axis=-1, keepdims=True).reshape(rows, 1)

        log = column(log_scales) + 32768.0 / PARTS
        unit = jnp.exp2(column(jnp.where(at_power, 1.0, 0.0))) * (1.0 / CODES)
        now = jnp.maximum(highest, log)
        keep, weight = jnp.exp(highest - now), jnp.exp(log - now)
        piece = o_all[part, 0:pairs].astype(jnp.int32).astype(F32).reshape(rows, dim)
        upper = upper * keep + (weight * unit) * piece
        lower = lower * keep + weight
        highest = now
    result = upper / lower
    for h in range(kvh):
        for t in range(steps):
            at = h * per + t * gsize
            out_ref[t, h] = result[at:at + gsize]

    settle(q_all.at[pl.ds(0, n - 1)], q_ss)
    settle(others(k_all), k_ss)
    settle(others(v_all), v_ss)
    settle(o_all.at[pl.ds(0, n - 1)], o_ss)


def solution(mesh):
    n = mesh.shape["sample"]

    def shards(queries, pk, pv, sk, sv, lengths, nk, nv):
        _, steps, heads, dim = queries.shape
        tokens, kvh, _ = pk.shape
        gsize = heads // kvh
        suffix = sk.shape[1]
        per = steps * gsize
        group = math.gcd(kvh, 4)
        chunk = math.gcd(suffix * kvh, 1024)
        chunks = suffix * kvh // chunk
        dma = pltpu.SemaphoreType.DMA
        out = pl.pallas_call(
            functools.partial(kernel, n, group, chunk),
            out_shape=jax.ShapeDtypeStruct((steps, kvh, gsize, dim), F32),
            in_specs=[pl.BlockSpec(memory_space=pltpu.SMEM)]
            + [pl.BlockSpec(memory_space=pltpu.HBM)] * 7,
            out_specs=pl.BlockSpec(memory_space=pltpu.VMEM),
            scratch_shapes=[
                pltpu.VMEM((steps, kvh, gsize, dim), BF16),
                pltpu.VMEM((tokens * kvh, dim), BF16),
                pltpu.VMEM((tokens * kvh, dim), BF16),
                pltpu.VMEM((tokens * kvh, dim), F32),
                pltpu.VMEM((kvh, tokens, dim), BF16),
                pltpu.VMEM((kvh, tokens, dim), BF16),
                pltpu.VMEM((n, steps, gsize, dim), BF16),
                pltpu.VMEM((kvh, tokens, dim), BF16),
                pltpu.VMEM((kvh, tokens, dim), BF16),
                pltpu.VMEM((suffix * kvh, dim), BF16),
                pltpu.VMEM((suffix * kvh, dim), BF16),
                pltpu.VMEM((steps, kvh, dim), BF16),
                pltpu.VMEM((steps, kvh, dim), BF16),
                pltpu.VMEM((chunks, kvh * per, chunk), F32),
                pltpu.VMEM((n, per // 2 + 1, 2, dim), I16),
                pltpu.VMEM((n, per // 2 + 1, 2, dim), I16),
                pltpu.VMEM((n * per, kvh * tokens), BF16),
                pltpu.VMEM((n * per, kvh * tokens), BF16),
                pltpu.VMEM((n * per, 1), F32),
                pltpu.VMEM((n * per, 1), F32),
                dma((5,)), dma((2 * chunks,)),
                pltpu.SemaphoreType.REGULAR, pltpu.SemaphoreType.REGULAR,
                dma, dma((n // kvh,)), dma, dma, dma, dma,
                dma, dma((n // kvh,)),
            ],
            compiler_params=pltpu.CompilerParams(
                collective_id=0, has_side_effects=True, vmem_limit_bytes=48 << 20
            ),
        )(lengths, *[pltpu.with_memory_space_constraint(x, pltpu.HBM) for x in (
            queries.reshape(steps, kvh, gsize, dim),
            pk.reshape(tokens * kvh, dim),
            pv.reshape(tokens * kvh, dim),
            sk.reshape(suffix * kvh, dim),
            sv.reshape(suffix * kvh, dim),
            nk.reshape(steps, kvh, dim),
            nv.reshape(steps, kvh, dim),
        )])
        return out.reshape(1, steps, heads, dim)

    spread = ("group", "sample")
    four = P(spread, None, None, None)
    three = P(spread, None, None)
    return jax.shard_map(
        shards, mesh=mesh,
        in_specs=(four, three, three, four, four, P(spread), four, four),
        out_specs=four, check_vma=False,
    )
```

```python
import functools
import math

import jax
import jax.numpy as jnp
from jax import lax
from jax.experimental import pallas as pl
from jax.experimental.pallas import tpu as pltpu
from jax.sharding import PartitionSpec as P

F32, BF16, I16 = jnp.float32, jnp.bfloat16, jnp.int16
CODES = 32767.0
PARTS = 65535.0


def rows_of(tiles):
    wide = tiles.astype(F32)
    return wide.reshape(math.prod(wide.shape[:-1]), wide.shape[-1])


def nt_dot(a, b):
    return lax.dot_general(a, b, (((1,), (1,)), ((), ())), preferred_element_type=F32)


def kernel(
    n, group,
    lens, q_hbm, pk_hbm, pv_hbm, sk_hbm, sv_hbm, nk_hbm, nv_hbm,
    out_ref,
    q_own, relay, pk, pv, wide, k_send, v_send, q_all, k_all, v_all, sk, sv, nk, nv, s_own, hide,
    o_send, o_all, w_high, w_low, log_all, total_all,
    local_sem, suf_sem, late_sem, block_sem, relay_ss, relay_rs, q_ss, q_rs, k_ss, k_rs, v_ss, v_rs, o_ss, o_rs,
):
    steps, kvh, gsize, dim = q_hbm.shape
    per = steps * gsize
    tokens = pk.shape[0] // kvh
    factor = 1.0 / math.sqrt(dim)
    me = lax.axis_index("sample")
    head = lax.rem(me, kvh)
    mine = lax.div(me, kvh)
    base = me - head
    couples, suffix = sk.shape[:2]
    blocks = n // kvh

    def remote(src, dst, ss, rs, dev):
        return pltpu.make_async_remote_copy(
            src_ref=src, dst_ref=dst, send_sem=ss, recv_sem=rs,
            device_id={"sample": dev}, device_id_type=pl.DeviceIdType.MESH,
        )

    def signal(sem, dev):
        pl.semaphore_signal(
            sem, inc=1, device_id={"sample": dev}, device_id_type=pl.DeviceIdType.MESH
        )

    def repeat(first, last, action):
        def body(d, _):
            action(d)
            return 0
        lax.fori_loop(first, last, body, 0)

    local = [
        pltpu.make_async_copy(a, b, local_sem.at[i])
        for i, (a, b) in enumerate(
            [(pk_hbm, pk), (pv_hbm, pv), (q_hbm, q_own), (nk_hbm, nk), (nv_hbm, nv)]
        )
    ]
    local[0].start()
    local[1].start()

    barrier = pltpu.get_barrier_semaphore()
    paired = blocks == 2 and kvh % 2 == 0 and kvh >= 4
    second = base > 0
    other = lax.rem(base + kvh, n)
    early = kvh - 2 if paired else kvh
    late = head >= early

    def to_early(action):
        repeat(jnp.where(late, 0, 1), early, lambda d: action(lax.rem(head + d, early)))

    def to_late(action):
        if paired:
            repeat(
                0, jnp.where(late, 1, 2), lambda d: action(early + lax.rem(head + 1 + d, 2))
            )

    def unless(skipped, action):
        pl.when(jnp.logical_not(skipped))(action)

    if paired:
        unless(late, lambda: to_early(lambda hd: signal(barrier, base + hd)))
        to_late(lambda hd: signal(barrier, base + hd))
        unless(second, lambda: repeat(early, kvh, lambda hd: signal(barrier, other + hd)))
    else:
        repeat(1, n, lambda d: signal(barrier, lax.rem(me + d, n)))

    def split(src, copy, dst, kept):
        copy.wait()
        wide[...] = src[...].astype(F32)
        for h in range(kvh):
            dst[h] = wide[pl.ds(h, tokens, stride=kvh), :].astype(BF16)
        kept[head] = wide[pl.ds(head, tokens, stride=kvh), :].astype(BF16)

    def settle(ref, sem):
        pltpu.make_async_copy(ref, ref, sem).wait()

    def others(ref):
        return ref.at[pl.ds(0, kvh - 1)]

    def send_q(dev):
        remote(q_hbm.at[:, lax.rem(dev, kvh)], q_all.at[me], q_ss, q_rs.at[mine], dev).start()

    def send_k(hd):
        remote(k_send.at[hd], k_all.at[head], k_ss, k_rs, base + hd).start()

    def send_v(hd):
        remote(v_send.at[hd], v_all.at[head], v_ss, v_rs, base + hd).start()

    def near_q(hd):
        send_q(base + hd)

    def far_q():
        repeat(0, n - kvh, lambda d: send_q(
            lax.rem(base + kvh + lax.rem(head + d, kvh) + lax.div(d, kvh) * kvh, n)
        ))

    half = kvh // 2
    outer = jnp.logical_not(second) & (head < half)
    inner = jnp.logical_not(second) & (head >= half)
    passes_to = lax.rem(head + half, kvh)
    must_ask = passes_to >= early

    def hand_over():
        remote(q_hbm, relay, q_ss, relay_rs, base + passes_to).start()

    def pass_on():
        settle(relay, relay_rs)

        def forward(d):
            hd = lax.rem(head + d, kvh)
            remote(
                relay.at[:, hd], q_all.at[base + passes_to], relay_ss, q_rs.at[mine], other + hd
            ).start()

        repeat(0, kvh, forward)

    if paired:
        @pl.when(late)
        def _():
            pl.semaphore_wait(barrier, jnp.where(second, n - 1, kvh - 1))
            repeat(0, early, lambda hd: signal(late_sem, base + hd))

            @pl.when(second)
            def _():
                repeat(0, kvh // 2, lambda d: signal(block_sem, other + 2 * d + head - early))

        unless(late, lambda: pl.semaphore_wait(barrier, early - 1))
    else:
        pl.semaphore_wait(barrier, n - 1)
    if paired:
        pl.when(outer & jnp.logical_not(must_ask))(hand_over)
    to_early(near_q)
    split(pk, local[0], k_send, k_all)
    to_early(send_k)
    for c in local[2:]:
        c.start()
    own_q = pltpu.make_async_copy(q_hbm.at[:, head], q_all.at[me], q_rs.at[mine])
    own_q.start()
    halves = [
        pltpu.make_async_copy(a.at[:, c], b.at[c], suf_sem.at[i * couples + c])
        for i, (a, b) in enumerate([(sk_hbm, sk), (sv_hbm, sv)]) for c in range(couples)
    ]
    for c in halves:
        c.start()
    if paired:
        unless(late, lambda: pl.semaphore_wait(late_sem, 2))
        pl.when(outer & must_ask)(hand_over)
        to_late(near_q)
        to_late(send_k)
        pl.when(second)(far_q)
    else:
        far_q()
    split(pv, local[1], v_send, v_all)
    to_early(send_v)
    to_late(send_v)
    if paired:
        @pl.when(jnp.logical_not(second))
        def _():
            pl.semaphore_wait(block_sem, 1)
            pl.when(inner)(far_q)

    for c in local[2:]:
        c.wait()
    rows = kvh * per
    q_rows = jnp.concatenate(
        [q_own[t, h].astype(F32) for h in range(kvh) for t in range(steps)], axis=0
    ).astype(BF16)
    length = lens[0]
    row = lax.broadcasted_iota(jnp.int32, (rows, 128), 0)
    lane = lax.broadcasted_iota(jnp.int32, (rows, 128), 1)
    lane_head = lax.rem(lane, kvh)
    match = (row >= lane_head * per) & (row < (lane_head + 1) * per)
    bias = jnp.where(match, 0.0, -jnp.inf).astype(F32)
    two = rows // couples
    key = lax.broadcasted_iota(jnp.int32, (two, 2 * suffix), 1)
    wide_row = lax.broadcasted_iota(jnp.int32, (two, 2 * suffix), 0)
    seen = (lax.rem(key, 2) == lax.div(wide_row, per)) & (lax.div(key, 2) < length)
    hide[...] = jnp.where(seen, 0.0, -jnp.inf).astype(F32)

    tops = []
    for c in range(couples):
        halves[c].wait()
        s = nt_dot(q_rows[c * two:(c + 1) * two], sk[c].reshape(2 * suffix, dim)) * factor + hide[...]
        s_own[c] = s
        tops.append(jnp.max(s, axis=-1, keepdims=True))
    top = jnp.concatenate(tops, axis=0)

    if paired:
        pl.when(inner)(pass_on)
    pad = jnp.zeros((128 - steps * kvh, dim), F32)
    new_k = jnp.concatenate([nk[j].astype(F32) for j in range(steps)] + [pad], axis=0).astype(BF16)
    new_v = jnp.concatenate([nv[j].astype(F32) for j in range(steps)] + [pad], axis=0).astype(BF16)
    step_of = lax.div(lax.rem(row, per), gsize)
    s_new = nt_dot(q_rows, new_k) * factor + bias
    s_new = jnp.where(lax.div(lane, kvh) <= step_of, s_new, -jnp.inf)
    own_max = jnp.maximum(top, jnp.max(s_new, axis=-1, keepdims=True))
    w_new = jnp.exp(s_new - own_max)
    own_total = jnp.sum(w_new, axis=-1, keepdims=True)
    own_sum = jnp.dot(w_new.astype(BF16), new_v, preferred_element_type=F32)
    totals, sums_of = [], []
    for c in range(couples):
        halves[couples + c].wait()
        w = jnp.exp(s_own[c] - own_max[c * two:(c + 1) * two])
        totals.append(jnp.sum(w, axis=-1, keepdims=True))
        sums_of.append(jnp.dot(
            w.astype(BF16), sv[c].reshape(2 * suffix, dim), preferred_element_type=F32
        ))
    own_total = own_total + jnp.concatenate(totals, axis=0)
    own_sum = own_sum + jnp.concatenate(sums_of, axis=0)

    settle(others(k_all), k_rs)
    keys = k_all[...].reshape(kvh * tokens, dim)
    groups = kvh // group
    span = group * per

    def place(block, i):
        first = block * kvh + i * group
        return first, pl.ds(pl.multiple_of(first * per, span), span)

    def weigh(block):
        settle(q_all.at[pl.ds(block * kvh, kvh)], q_rs.at[block])

        if True:
            first = block * kvh
            at = pl.ds(pl.multiple_of(first * per, kvh * per), kvh * per)
            q_block = rows_of(q_all[pl.ds(first, kvh)]).astype(BF16)
            s = nt_dot(q_block, keys)
            m = jnp.max(s, axis=-1, keepdims=True)
            w = jnp.exp2((s - m) * (factor * math.log2(math.e)))
            total = jnp.sum(w, axis=-1, keepdims=True)
            high = w.astype(BF16)
            w_high[at] = high
            w_low[at] = (w - high.astype(F32)).astype(BF16)
            total_all[at] = total
            log_all[at] = m * factor + jnp.log(total)


    repeat(0, blocks, lambda b: weigh(lax.rem(mine + b, blocks)))

    settle(others(v_all), v_rs)
    values = v_all[...].reshape(kvh * tokens, dim)
    diag_row = lax.broadcasted_iota(jnp.int32, (per, 128), 0)
    diag_lane = lax.broadcasted_iota(jnp.int32, (per, 128), 1)
    at_whole = diag_lane == diag_row
    at_part = diag_lane == diag_row + 32
    at_power = diag_lane == diag_row + 64
    pairs = per // 2

    def emit(block):
        def body(i):
            first, at = place(block, i)
            sums = jnp.dot(w_high[at], values, preferred_element_type=F32) + jnp.dot(
                w_low[at], values, preferred_element_type=F32
            )
            total = total_all[at]
            largest = jnp.max(jnp.abs(sums), axis=-1, keepdims=True)
            power = jnp.ceil(jnp.log2(jnp.maximum(largest / total, 1e-30)))
            code = jnp.round(sums * (CODES * jnp.exp2(-power) / total))
            log = log_all[at]
            whole = jnp.floor(log)
            part = jnp.round((log - whole) * PARTS) - 32768.0

            def lanes(column):
                return jnp.broadcast_to(column, (span, 128)).reshape(group, per, 128)

            facts = jnp.where(at_whole[None], lanes(whole), jnp.where(
                at_part[None], lanes(part), jnp.where(at_power[None], lanes(power), 0.0)
            ))
            facts = jnp.broadcast_to(jnp.sum(facts, axis=1, keepdims=True), (group, 2, 128))
            here = pl.ds(first, group)
            o_send[here, 0:pairs] = code.astype(jnp.int32).astype(I16).reshape(group, pairs, 2, dim)
            o_send[here, pairs:] = facts.astype(jnp.int32).astype(I16).reshape(group, 1, 2, dim)
            for j in range(group):
                dev = first + j

                @pl.when(dev != me)
                def _():
                    remote(o_send.at[dev], o_all.at[me], o_ss, o_rs.at[mine], dev).start()

                @pl.when(dev == me)
                def _():
                    pltpu.make_async_copy(o_send.at[dev], o_all.at[dev], o_rs.at[mine]).start()

        repeat(0, groups, body)

    repeat(1, blocks + 1, lambda b: emit(lax.rem(mine + b, blocks)))

    log_scales = jnp.where(at_whole, 1.0, jnp.where(at_part, 1.0 / PARTS, 0.0))
    highest, upper, lower = own_max, own_sum, own_total
    for r in range(blocks):
        part = pl.ds(r * kvh, kvh)
        settle(o_all.at[part], o_rs.at[r])
        facts = o_all[part, pairs:].astype(jnp.int32).astype(F32)
        spread = jnp.broadcast_to(facts.reshape(kvh, 2, 128)[:, 0:1], (kvh, per, 128))

        def column(scales):
            return jnp.sum(spread * scales[None], axis=-1, keepdims=True).reshape(rows, 1)

        log = column(log_scales) + 32768.0 / PARTS
        unit = jnp.exp2(column(jnp.where(at_power, 1.0, 0.0))) * (1.0 / CODES)
        now = jnp.maximum(highest, log)
        keep, weight = jnp.exp(highest - now), jnp.exp(log - now)
        piece = o_all[part, 0:pairs].astype(jnp.int32).astype(F32).reshape(rows, dim)
        upper = upper * keep + (weight * unit) * piece
        lower = lower * keep + weight
        highest = now
    result = upper / lower
    for h in range(kvh):
        for t in range(steps):
            at = h * per + t * gsize
            out_ref[t, h] = result[at:at + gsize]

    settle(q_all.at[pl.ds(0, n - 1)], q_ss)
    if paired:
        pl.when(inner)(lambda: settle(q_all.at[pl.ds(0, kvh)], relay_ss))
    settle(others(k_all), k_ss)
    settle(others(v_all), v_ss)
    settle(o_all.at[pl.ds(0, n - 1)], o_ss)


def solution(mesh):
    n = mesh.shape["sample"]

    def shards(queries, pk, pv, sk, sv, lengths, nk, nv):
        _, steps, heads, dim = queries.shape
        tokens, kvh, _ = pk.shape
        gsize = heads // kvh
        suffix = sk.shape[1]
        per = steps * gsize
        group = math.gcd(kvh, 4)
        dma = pltpu.SemaphoreType.DMA
        out = pl.pallas_call(
            functools.partial(kernel, n, group),
            out_shape=jax.ShapeDtypeStruct((steps, kvh, gsize, dim), F32),
            in_specs=[pl.BlockSpec(memory_space=pltpu.SMEM)]
            + [pl.BlockSpec(memory_space=pltpu.HBM)] * 7,
            out_specs=pl.BlockSpec(memory_space=pltpu.VMEM),
            scratch_shapes=[
                pltpu.VMEM((steps, kvh, gsize, dim), BF16),
                pltpu.VMEM((steps, kvh, gsize, dim), BF16),
                pltpu.VMEM((tokens * kvh, dim), BF16),
                pltpu.VMEM((tokens * kvh, dim), BF16),
                pltpu.VMEM((tokens * kvh, dim), F32),
                pltpu.VMEM((kvh, tokens, dim), BF16),
                pltpu.VMEM((kvh, tokens, dim), BF16),
                pltpu.VMEM((n, steps, gsize, dim), BF16),
                pltpu.VMEM((kvh, tokens, dim), BF16),
                pltpu.VMEM((kvh, tokens, dim), BF16),
                pltpu.VMEM((kvh // 2, suffix, 2, dim), BF16),
                pltpu.VMEM((kvh // 2, suffix, 2, dim), BF16),
                pltpu.VMEM((steps, kvh, dim), BF16),
                pltpu.VMEM((steps, kvh, dim), BF16),
                pltpu.VMEM((kvh // 2, 2 * per, 2 * suffix), F32),
                pltpu.VMEM((2 * per, 2 * suffix), F32),
                pltpu.VMEM((n, per // 2 + 1, 2, dim), I16),
                pltpu.VMEM((n, per // 2 + 1, 2, dim), I16),
                pltpu.VMEM((n * per, kvh * tokens), BF16),
                pltpu.VMEM((n * per, kvh * tokens), BF16),
                pltpu.VMEM((n * per, 1), F32),
                pltpu.VMEM((n * per, 1), F32),
                dma((5,)), dma((kvh,)),
                pltpu.SemaphoreType.REGULAR, pltpu.SemaphoreType.REGULAR, dma, dma,
                dma, dma((n // kvh,)), dma, dma, dma, dma,
                dma, dma((n // kvh,)),
            ],
            compiler_params=pltpu.CompilerParams(
                collective_id=0, has_side_effects=True, vmem_limit_bytes=48 << 20
            ),
        )(lengths, *[pltpu.with_memory_space_constraint(x, pltpu.HBM) for x in (
            queries.reshape(steps, kvh, gsize, dim),
            pk.reshape(tokens * kvh, dim),
            pv.reshape(tokens * kvh, dim),
            sk.reshape(suffix, kvh // 2, 2, dim),
            sv.reshape(suffix, kvh // 2, 2, dim),
            nk.reshape(steps, kvh, dim),
            nv.reshape(steps, kvh, dim),
        )])
        return out.reshape(1, steps, heads, dim)

    spread = ("group", "sample")
    four = P(spread, None, None, None)
    three = P(spread, None, None)
    return jax.shard_map(
        shards, mesh=mesh,
        in_specs=(four, three, three, four, four, P(spread), four, four),
        out_specs=four, check_vma=False,
    )
```

```python
import functools
import math

import jax
import jax.numpy as jnp
from jax import lax
from jax.experimental import pallas as pl
from jax.experimental.pallas import tpu as pltpu
from jax.sharding import PartitionSpec as P

F32, BF16, I16 = jnp.float32, jnp.bfloat16, jnp.int16
STEPS_OF_CODE = 32767.0


def rows_of(tiles):
    wide = tiles.astype(F32)
    return wide.reshape(math.prod(wide.shape[:-1]), wide.shape[-1])


def nt_dot(a, b):
    return lax.dot_general(a, b, (((1,), (1,)), ((), ())), preferred_element_type=F32)


def kernel(
    n, group,
    lens, q_hbm, pk_hbm, pv_hbm, sk_hbm, sv_hbm, nk_hbm, nv_hbm,
    out_ref,
    q_own, pk, pv, wide, k_send, v_send, q_all, k_all, v_all, sk, sv, nk, nv, s_own, hide,
    o_send, l_send, o_all, l_all, w_high, w_low, log_all, total_all,
    local_sem, suf_sem, late_sem, block_sem, q_ss, q_rs, k_ss, k_rs, v_ss, v_rs, o_ss, o_rs, l_ss, l_rs,
):
    steps, kvh, gsize, dim = q_hbm.shape
    per = steps * gsize
    tokens = pk.shape[0] // kvh
    factor = 1.0 / math.sqrt(dim)
    me = lax.axis_index("sample")
    head = lax.rem(me, kvh)
    mine = lax.div(me, kvh)
    base = me - head
    couples, suffix = sk.shape[:2]
    blocks = n // kvh

    def remote(src, dst, ss, rs, dev):
        return pltpu.make_async_remote_copy(
            src_ref=src, dst_ref=dst, send_sem=ss, recv_sem=rs,
            device_id={"sample": dev}, device_id_type=pl.DeviceIdType.MESH,
        )

    def signal(sem, dev):
        pl.semaphore_signal(
            sem, inc=1, device_id={"sample": dev}, device_id_type=pl.DeviceIdType.MESH
        )

    def repeat(first, last, action):
        def body(d, _):
            action(d)
            return 0
        lax.fori_loop(first, last, body, 0)

    local = [
        pltpu.make_async_copy(a, b, local_sem.at[i])
        for i, (a, b) in enumerate(
            [(pk_hbm, pk), (pv_hbm, pv), (q_hbm, q_own), (nk_hbm, nk), (nv_hbm, nv)]
        )
    ]
    local[0].start()

    barrier = pltpu.get_barrier_semaphore()
    paired = blocks == 2 and kvh % 2 == 0 and kvh >= 4
    second = base > 0
    other = lax.rem(base + kvh, n)
    early = kvh - 2 if paired else kvh
    late = head >= early

    def to_early(action):
        repeat(jnp.where(late, 0, 1), early, lambda d: action(lax.rem(head + d, early)))

    def to_late(action):
        if paired:
            repeat(
                0, jnp.where(late, 1, 2), lambda d: action(early + lax.rem(head + 1 + d, 2))
            )

    def unless(skipped, action):
        pl.when(jnp.logical_not(skipped))(action)

    if paired:
        unless(late, lambda: to_early(lambda hd: signal(barrier, base + hd)))
        to_late(lambda hd: signal(barrier, base + hd))
        unless(second, lambda: repeat(early, kvh, lambda hd: signal(barrier, other + hd)))
    else:
        repeat(1, n, lambda d: signal(barrier, lax.rem(me + d, n)))

    for c in local[1:]:
        c.start()
    own_q = pltpu.make_async_copy(q_hbm.at[:, head], q_all.at[me], q_rs.at[mine])
    own_q.start()
    halves = [
        pltpu.make_async_copy(a.at[:, c], b.at[c], suf_sem.at[i * couples + c])
        for i, (a, b) in enumerate([(sk_hbm, sk), (sv_hbm, sv)]) for c in range(couples)
    ]
    for c in halves:
        c.start()

    def split(src, copy, dst, kept):
        copy.wait()
        wide[...] = src[...].astype(F32)
        for h in range(kvh):
            dst[h] = wide[pl.ds(h, tokens, stride=kvh), :].astype(BF16)
        kept[head] = wide[pl.ds(head, tokens, stride=kvh), :].astype(BF16)

    def send_q(dev):
        remote(q_hbm.at[:, lax.rem(dev, kvh)], q_all.at[me], q_ss, q_rs.at[mine], dev).start()

    def send_k(hd):
        remote(k_send.at[hd], k_all.at[head], k_ss, k_rs, base + hd).start()

    def send_v(hd):
        remote(v_send.at[hd], v_all.at[head], v_ss, v_rs, base + hd).start()

    def near_q(hd):
        send_q(base + hd)

    def far_q():
        repeat(0, n - kvh, lambda d: send_q(
            lax.rem(base + kvh + lax.rem(head + d, kvh) + lax.div(d, kvh) * kvh, n)
        ))

    if paired:
        @pl.when(late)
        def _():
            pl.semaphore_wait(barrier, jnp.where(second, n - 1, kvh - 1))
            repeat(0, early, lambda hd: signal(late_sem, base + hd))

            @pl.when(second)
            def _():
                repeat(0, kvh // 2, lambda d: signal(block_sem, other + 2 * d + head - early))

        unless(late, lambda: pl.semaphore_wait(barrier, early - 1))
    else:
        pl.semaphore_wait(barrier, n - 1)
    to_early(near_q)
    split(pk, local[0], k_send, k_all)
    to_early(send_k)
    if paired:
        unless(late, lambda: pl.semaphore_wait(late_sem, 2))
        to_late(near_q)
        to_late(send_k)
        pl.when(second)(far_q)
    else:
        far_q()
    split(pv, local[1], v_send, v_all)
    if paired:
        @pl.when(jnp.logical_not(second))
        def _():
            pl.semaphore_wait(block_sem, 1)
            far_q()
    to_early(send_v)
    to_late(send_v)

    for c in local[2:]:
        c.wait()
    rows = kvh * per
    q_rows = jnp.concatenate(
        [q_own[t, h].astype(F32) for h in range(kvh) for t in range(steps)], axis=0
    ).astype(BF16)
    length = lens[0]
    row = lax.broadcasted_iota(jnp.int32, (rows, 128), 0)
    lane = lax.broadcasted_iota(jnp.int32, (rows, 128), 1)
    lane_head = lax.rem(lane, kvh)
    match = (row >= lane_head * per) & (row < (lane_head + 1) * per)
    bias = jnp.where(match, 0.0, -jnp.inf).astype(F32)
    two = rows // couples
    key = lax.broadcasted_iota(jnp.int32, (two, 2 * suffix), 1)
    wide_row = lax.broadcasted_iota(jnp.int32, (two, 2 * suffix), 0)
    seen = (lax.rem(key, 2) == lax.div(wide_row, per)) & (lax.div(key, 2) < length)
    hide[...] = jnp.where(seen, 0.0, -jnp.inf).astype(F32)

    tops = []
    for c in range(couples):
        halves[c].wait()
        s = nt_dot(q_rows[c * two:(c + 1) * two], sk[c].reshape(2 * suffix, dim)) * factor + hide[...]
        s_own[c] = s
        tops.append(jnp.max(s, axis=-1, keepdims=True))
    top = jnp.concatenate(tops, axis=0)

    pad = jnp.zeros((128 - steps * kvh, dim), F32)
    new_k = jnp.concatenate([nk[j].astype(F32) for j in range(steps)] + [pad], axis=0).astype(BF16)
    new_v = jnp.concatenate([nv[j].astype(F32) for j in range(steps)] + [pad], axis=0).astype(BF16)
    step_of = lax.div(lax.rem(row, per), gsize)
    s_new = nt_dot(q_rows, new_k) * factor + bias
    s_new = jnp.where(lax.div(lane, kvh) <= step_of, s_new, -jnp.inf)
    own_max = jnp.maximum(top, jnp.max(s_new, axis=-1, keepdims=True))
    w_new = jnp.exp(s_new - own_max)
    own_total = jnp.sum(w_new, axis=-1, keepdims=True)
    own_sum = jnp.dot(w_new.astype(BF16), new_v, preferred_element_type=F32)
    totals, sums_of = [], []
    for c in range(couples):
        halves[couples + c].wait()
        w = jnp.exp(s_own[c] - own_max[c * two:(c + 1) * two])
        totals.append(jnp.sum(w, axis=-1, keepdims=True))
        sums_of.append(jnp.dot(
            w.astype(BF16), sv[c].reshape(2 * suffix, dim), preferred_element_type=F32
        ))
    own_total = own_total + jnp.concatenate(totals, axis=0)
    own_sum = own_sum + jnp.concatenate(sums_of, axis=0)

    def settle(ref, sem):
        pltpu.make_async_copy(ref, ref, sem).wait()

    def others(ref):
        return ref.at[pl.ds(0, kvh - 1)]

    settle(others(k_all), k_rs)
    keys = k_all[...].reshape(kvh * tokens, dim)
    groups = kvh // group
    span = group * per

    def place(block, i):
        first = block * kvh + i * group
        return first, pl.ds(pl.multiple_of(first * per, span), span)

    def weigh(block):
        settle(q_all.at[pl.ds(block * kvh, kvh)], q_rs.at[block])

        def body(i):
            first, at = place(block, i)
            q_block = rows_of(q_all[pl.ds(first, group)]).astype(BF16)
            s = nt_dot(q_block, keys) * factor
            m = jnp.max(s, axis=-1, keepdims=True)
            w = jnp.exp(s - m)
            total = jnp.sum(w, axis=-1, keepdims=True)
            high = w.astype(BF16)
            w_high[at] = high
            w_low[at] = (w - high.astype(F32)).astype(BF16)
            total_all[at] = total
            log_all[at] = m + jnp.log(total)

        repeat(0, groups, body)

    repeat(0, blocks, lambda b: weigh(lax.rem(mine + b, blocks)))

    settle(others(v_all), v_rs)
    values = v_all[...].reshape(kvh * tokens, dim)
    diag_row = lax.broadcasted_iota(jnp.int32, (per, 128), 0)
    diag_lane = lax.broadcasted_iota(jnp.int32, (per, 128), 1)
    at_log = diag_lane == diag_row
    at_unit = diag_lane == diag_row + 64

    def emit(block):
        def body(i):
            first, at = place(block, i)
            sums = jnp.dot(w_high[at], values, preferred_element_type=F32) + jnp.dot(
                w_low[at], values, preferred_element_type=F32
            )
            largest = jnp.maximum(jnp.max(jnp.abs(sums), axis=-1, keepdims=True), 1e-30)
            code = jnp.round(sums * (STEPS_OF_CODE / largest)).astype(jnp.int32).astype(I16)
            o_send[pl.ds(first, group)] = code.reshape(group, steps, gsize, dim)
            unit = largest / (STEPS_OF_CODE * total_all[at])
            both = jnp.where(
                at_log[None],
                jnp.broadcast_to(log_all[at], (span, 128)).reshape(group, per, 128),
                jnp.where(
                    at_unit[None],
                    jnp.broadcast_to(unit, (span, 128)).reshape(group, per, 128),
                    0.0,
                ),
            )
            l_send[pl.ds(first, group)] = jnp.sum(both, axis=1, keepdims=True)
            for j in range(group):
                dev = first + j

                @pl.when(dev != me)
                def _():
                    remote(o_send.at[dev], o_all.at[me], o_ss, o_rs.at[mine], dev).start()
                    remote(l_send.at[dev], l_all.at[me], l_ss, l_rs.at[mine], dev).start()

                @pl.when(dev == me)
                def _():
                    pltpu.make_async_copy(o_send.at[dev], o_all.at[dev], o_rs.at[mine]).start()
                    pltpu.make_async_copy(l_send.at[dev], l_all.at[dev], l_rs.at[mine]).start()

        repeat(0, groups, body)

    repeat(1, blocks + 1, lambda b: emit(b - 1))

    highest, upper, lower = own_max, own_sum, own_total
    for r in range(blocks):
        part = pl.ds(r * kvh, kvh)
        settle(l_all.at[part], l_rs.at[r])
        spread = jnp.broadcast_to(l_all[part], (kvh, per, 128))

        def column(where):
            return jnp.sum(
                jnp.where(where[None], spread, 0.0), axis=-1, keepdims=True
            ).reshape(rows, 1)

        log = column(at_log)
        unit = column(at_unit)
        now = jnp.maximum(highest, log)
        keep, weight = jnp.exp(highest - now), jnp.exp(log - now)
        settle(o_all.at[part], o_rs.at[r])
        piece = o_all[part].astype(jnp.int32).astype(F32).reshape(rows, dim)
        upper = upper * keep + (weight * unit) * piece
        lower = lower * keep + weight
        highest = now
    result = upper / lower
    for h in range(kvh):
        for t in range(steps):
            at = h * per + t * gsize
            out_ref[t, h] = result[at:at + gsize]

    settle(q_all.at[pl.ds(0, n - 1)], q_ss)
    settle(others(k_all), k_ss)
    settle(others(v_all), v_ss)
    settle(o_all.at[pl.ds(0, n - 1)], o_ss)
    settle(l_all.at[pl.ds(0, n - 1)], l_ss)


def solution(mesh):
    n = mesh.shape["sample"]

    def shards(queries, pk, pv, sk, sv, lengths, nk, nv):
        _, steps, heads, dim = queries.shape
        tokens, kvh, _ = pk.shape
        gsize = heads // kvh
        suffix = sk.shape[1]
        per = steps * gsize
        group = math.gcd(kvh, 4)
        dma = pltpu.SemaphoreType.DMA
        out = pl.pallas_call(
            functools.partial(kernel, n, group),
            out_shape=jax.ShapeDtypeStruct((steps, kvh, gsize, dim), F32),
            in_specs=[pl.BlockSpec(memory_space=pltpu.SMEM)]
            + [pl.BlockSpec(memory_space=pltpu.HBM)] * 7,
            out_specs=pl.BlockSpec(memory_space=pltpu.VMEM),
            scratch_shapes=[
                pltpu.VMEM((steps, kvh, gsize, dim), BF16),
                pltpu.VMEM((tokens * kvh, dim), BF16),
                pltpu.VMEM((tokens * kvh, dim), BF16),
                pltpu.VMEM((tokens * kvh, dim), F32),
                pltpu.VMEM((kvh, tokens, dim), BF16),
                pltpu.VMEM((kvh, tokens, dim), BF16),
                pltpu.VMEM((n, steps, gsize, dim), BF16),
                pltpu.VMEM((kvh, tokens, dim), BF16),
                pltpu.VMEM((kvh, tokens, dim), BF16),
                pltpu.VMEM((kvh // 2, suffix, 2, dim), BF16),
                pltpu.VMEM((kvh // 2, suffix, 2, dim), BF16),
                pltpu.VMEM((steps, kvh, dim), BF16),
                pltpu.VMEM((steps, kvh, dim), BF16),
                pltpu.VMEM((kvh // 2, 2 * per, 2 * suffix), F32),
                pltpu.VMEM((2 * per, 2 * suffix), F32),
                pltpu.VMEM((n, steps, gsize, dim), I16),
                pltpu.VMEM((n, 1, 128), F32),
                pltpu.VMEM((n, steps, gsize, dim), I16),
                pltpu.VMEM((n, 1, 128), F32),
                pltpu.VMEM((n * per, kvh * tokens), BF16),
                pltpu.VMEM((n * per, kvh * tokens), BF16),
                pltpu.VMEM((n * per, 1), F32),
                pltpu.VMEM((n * per, 1), F32),
                dma((5,)), dma((kvh,)),
                pltpu.SemaphoreType.REGULAR, pltpu.SemaphoreType.REGULAR,
                dma, dma((n // kvh,)), dma, dma, dma, dma,
                dma, dma((n // kvh,)), dma, dma((n // kvh,)),
            ],
            compiler_params=pltpu.CompilerParams(
                collective_id=0, has_side_effects=True, vmem_limit_bytes=48 << 20
            ),
        )(lengths, *[pltpu.with_memory_space_constraint(x, pltpu.HBM) for x in (
            queries.reshape(steps, kvh, gsize, dim),
            pk.reshape(tokens * kvh, dim),
            pv.reshape(tokens * kvh, dim),
            sk.reshape(suffix, kvh // 2, 2, dim),
            sv.reshape(suffix, kvh // 2, 2, dim),
            nk.reshape(steps, kvh, dim),
            nv.reshape(steps, kvh, dim),
        )])
        return out.reshape(1, steps, heads, dim)

    spread = ("group", "sample")
    four = P(spread, None, None, None)
    three = P(spread, None, None)
    return jax.shard_map(
        shards, mesh=mesh,
        in_specs=(four, three, three, four, four, P(spread), four, four),
        out_specs=four, check_vma=False,
    )
```

```python
import functools
import math

import jax
import jax.numpy as jnp
from jax import lax
from jax.experimental import pallas as pl
from jax.experimental.pallas import tpu as pltpu
from jax.sharding import PartitionSpec as P

F32, BF16, I16 = jnp.float32, jnp.bfloat16, jnp.int16
STEPS_OF_CODE = 32767.0


def rows_of(tiles):
    wide = tiles.astype(F32)
    return wide.reshape(math.prod(wide.shape[:-1]), wide.shape[-1])


def nt_dot(a, b):
    return lax.dot_general(a, b, (((1,), (1,)), ((), ())), preferred_element_type=F32)


def kernel(
    n, group,
    lens, q_hbm, pk_hbm, pv_hbm, sk_hbm, sv_hbm, nk_hbm, nv_hbm,
    out_ref,
    q_own, pk, pv, wide, k_send, v_send, q_all, k_all, v_all, sk, sv, nk, nv, s_own, hide,
    o_send, l_send, o_all, l_all, w_high, w_low, log_all, total_all,
    local_sem, suf_sem, late_sem, block_sem, q_ss, q_rs, k_ss, k_rs, v_ss, v_rs, o_ss, o_rs, l_ss, l_rs,
):
    steps, kvh, gsize, dim = q_hbm.shape
    per = steps * gsize
    tokens = pk.shape[0] // kvh
    factor = 1.0 / math.sqrt(dim)
    me = lax.axis_index("sample")
    head = lax.rem(me, kvh)
    mine = lax.div(me, kvh)
    base = me - head
    couples, suffix = sk.shape[:2]
    blocks = n // kvh

    def remote(src, dst, ss, rs, dev):
        return pltpu.make_async_remote_copy(
            src_ref=src, dst_ref=dst, send_sem=ss, recv_sem=rs,
            device_id={"sample": dev}, device_id_type=pl.DeviceIdType.MESH,
        )

    def signal(sem, dev):
        pl.semaphore_signal(
            sem, inc=1, device_id={"sample": dev}, device_id_type=pl.DeviceIdType.MESH
        )

    def repeat(first, last, action):
        def body(d, _):
            action(d)
            return 0
        lax.fori_loop(first, last, body, 0)

    local = [
        pltpu.make_async_copy(a, b, local_sem.at[i])
        for i, (a, b) in enumerate(
            [(pk_hbm, pk), (pv_hbm, pv), (q_hbm, q_own), (nk_hbm, nk), (nv_hbm, nv)]
        )
    ]
    local[0].start()

    barrier = pltpu.get_barrier_semaphore()
    paired = blocks == 2 and kvh % 2 == 0 and kvh >= 4
    second = base > 0
    other = lax.rem(base + kvh, n)
    early = kvh - 2 if paired else kvh
    late = head >= early

    def to_early(action):
        repeat(jnp.where(late, 0, 1), early, lambda d: action(lax.rem(head + d, early)))

    def to_late(action):
        if paired:
            repeat(
                0, jnp.where(late, 1, 2), lambda d: action(early + lax.rem(head + 1 + d, 2))
            )

    def unless(skipped, action):
        pl.when(jnp.logical_not(skipped))(action)

    if paired:
        unless(late, lambda: to_early(lambda hd: signal(barrier, base + hd)))
        to_late(lambda hd: signal(barrier, base + hd))
        unless(second, lambda: repeat(early, kvh, lambda hd: signal(barrier, other + hd)))
    else:
        repeat(1, n, lambda d: signal(barrier, lax.rem(me + d, n)))

    for c in local[1:]:
        c.start()
    own_q = pltpu.make_async_copy(q_hbm.at[:, head], q_all.at[me], q_rs.at[mine])
    own_q.start()
    halves = [
        pltpu.make_async_copy(a.at[:, c], b.at[c], suf_sem.at[i * couples + c])
        for i, (a, b) in enumerate([(sk_hbm, sk), (sv_hbm, sv)]) for c in range(couples)
    ]
    for c in halves:
        c.start()

    def split(src, copy, dst, kept):
        copy.wait()
        wide[...] = src[...].astype(F32)
        for h in range(kvh):
            dst[h] = wide[pl.ds(h, tokens, stride=kvh), :].astype(BF16)
        kept[head] = wide[pl.ds(head, tokens, stride=kvh), :].astype(BF16)

    def send_q(dev):
        remote(q_hbm.at[:, lax.rem(dev, kvh)], q_all.at[me], q_ss, q_rs.at[mine], dev).start()

    def send_k(hd):
        remote(k_send.at[hd], k_all.at[head], k_ss, k_rs, base + hd).start()

    def send_v(hd):
        remote(v_send.at[hd], v_all.at[head], v_ss, v_rs, base + hd).start()

    def near_q(hd):
        send_q(base + hd)

    def far_q():
        repeat(0, n - kvh, lambda d: send_q(
            lax.rem(base + kvh + lax.rem(head + d, kvh) + lax.div(d, kvh) * kvh, n)
        ))

    if paired:
        @pl.when(late)
        def _():
            pl.semaphore_wait(barrier, jnp.where(second, n - 1, kvh - 1))
            repeat(0, early, lambda hd: signal(late_sem, base + hd))

            @pl.when(second)
            def _():
                repeat(0, kvh // 2, lambda d: signal(block_sem, other + 2 * d + head - early))

        unless(late, lambda: pl.semaphore_wait(barrier, early - 1))
    else:
        pl.semaphore_wait(barrier, n - 1)
    to_early(near_q)
    split(pk, local[0], k_send, k_all)
    to_early(send_k)
    if paired:
        unless(late, lambda: pl.semaphore_wait(late_sem, 2))
        to_late(near_q)
        to_late(send_k)
        pl.when(second)(far_q)
    else:
        far_q()
    split(pv, local[1], v_send, v_all)
    if paired:
        @pl.when(jnp.logical_not(second))
        def _():
            pl.semaphore_wait(block_sem, 1)
            far_q()
    to_early(send_v)
    to_late(send_v)

    for c in local[2:]:
        c.wait()
    rows = kvh * per
    q_rows = jnp.concatenate(
        [q_own[t, h].astype(F32) for h in range(kvh) for t in range(steps)], axis=0
    ).astype(BF16)
    length = lens[0]
    row = lax.broadcasted_iota(jnp.int32, (rows, 128), 0)
    lane = lax.broadcasted_iota(jnp.int32, (rows, 128), 1)
    lane_head = lax.rem(lane, kvh)
    match = (row >= lane_head * per) & (row < (lane_head + 1) * per)
    bias = jnp.where(match, 0.0, -jnp.inf).astype(F32)
    two = rows // couples
    key = lax.broadcasted_iota(jnp.int32, (two, 2 * suffix), 1)
    wide_row = lax.broadcasted_iota(jnp.int32, (two, 2 * suffix), 0)
    seen = (lax.rem(key, 2) == lax.div(wide_row, per)) & (lax.div(key, 2) < length)
    hide[...] = jnp.where(seen, 0.0, -jnp.inf).astype(F32)

    tops = []
    for c in range(couples):
        halves[c].wait()
        s = nt_dot(q_rows[c * two:(c + 1) * two], sk[c].reshape(2 * suffix, dim)) * factor + hide[...]
        s_own[c] = s
        tops.append(jnp.max(s, axis=-1, keepdims=True))
    top = jnp.concatenate(tops, axis=0)

    pad = jnp.zeros((128 - steps * kvh, dim), F32)
    new_k = jnp.concatenate([nk[j].astype(F32) for j in range(steps)] + [pad], axis=0).astype(BF16)
    new_v = jnp.concatenate([nv[j].astype(F32) for j in range(steps)] + [pad], axis=0).astype(BF16)
    step_of = lax.div(lax.rem(row, per), gsize)
    s_new = nt_dot(q_rows, new_k) * factor + bias
    s_new = jnp.where(lax.div(lane, kvh) <= step_of, s_new, -jnp.inf)
    own_max = jnp.maximum(top, jnp.max(s_new, axis=-1, keepdims=True))
    w_new = jnp.exp(s_new - own_max)
    own_total = jnp.sum(w_new, axis=-1, keepdims=True)
    own_sum = jnp.dot(w_new.astype(BF16), new_v, preferred_element_type=F32)
    totals, sums_of = [], []
    for c in range(couples):
        halves[couples + c].wait()
        w = jnp.exp(s_own[c] - own_max[c * two:(c + 1) * two])
        totals.append(jnp.sum(w, axis=-1, keepdims=True))
        sums_of.append(jnp.dot(
            w.astype(BF16), sv[c].reshape(2 * suffix, dim), preferred_element_type=F32
        ))
    own_total = own_total + jnp.concatenate(totals, axis=0)
    own_sum = own_sum + jnp.concatenate(sums_of, axis=0)

    def settle(ref, sem):
        pltpu.make_async_copy(ref, ref, sem).wait()

    def others(ref):
        return ref.at[pl.ds(0, kvh - 1)]

    settle(others(k_all), k_rs)
    keys = k_all[...].reshape(kvh * tokens, dim)
    groups = kvh // group
    span = group * per

    def place(block, i):
        first = block * kvh + i * group
        return first, pl.ds(pl.multiple_of(first * per, span), span)

    def weigh(block):
        settle(q_all.at[pl.ds(block * kvh, kvh)], q_rs.at[block])

        if True:
            first = block * kvh
            at = pl.ds(pl.multiple_of(first * per, kvh * per), kvh * per)
            q_block = rows_of(q_all[pl.ds(first, kvh)]).astype(BF16)
            s = nt_dot(q_block, keys)
            m = jnp.max(s, axis=-1, keepdims=True)
            w = jnp.exp2((s - m) * (factor * math.log2(math.e)))
            total = jnp.sum(w, axis=-1, keepdims=True)
            high = w.astype(BF16)
            w_high[at] = high
            w_low[at] = (w - high.astype(F32)).astype(BF16)
            total_all[at] = total
            log_all[at] = m * factor + jnp.log(total)


    repeat(0, blocks, lambda b: weigh(lax.rem(mine + b, blocks)))

    settle(others(v_all), v_rs)
    values = v_all[...].reshape(kvh * tokens, dim)
    diag_row = lax.broadcasted_iota(jnp.int32, (per, 128), 0)
    diag_lane = lax.broadcasted_iota(jnp.int32, (per, 128), 1)
    at_log = diag_lane == diag_row
    at_unit = diag_lane == diag_row + 64

    def emit(block):
        def body(i):
            first, at = place(block, i)
            sums = jnp.dot(w_high[at], values, preferred_element_type=F32) + jnp.dot(
                w_low[at], values, preferred_element_type=F32
            )
            largest = jnp.maximum(jnp.max(jnp.abs(sums), axis=-1, keepdims=True), 1e-30)
            code = jnp.round(sums * (STEPS_OF_CODE / largest)).astype(jnp.int32).astype(I16)
            o_send[pl.ds(first, group)] = code.reshape(group, steps, gsize, dim)
            unit = largest / (STEPS_OF_CODE * total_all[at])
            both = jnp.where(
                at_log[None],
                jnp.broadcast_to(log_all[at], (span, 128)).reshape(group, per, 128),
                jnp.where(
                    at_unit[None],
                    jnp.broadcast_to(unit, (span, 128)).reshape(group, per, 128),
                    0.0,
                ),
            )
            l_send[pl.ds(first, group)] = jnp.sum(both, axis=1, keepdims=True)
            for j in range(group):
                dev = first + j

                @pl.when(dev != me)
                def _():
                    remote(o_send.at[dev], o_all.at[me], o_ss, o_rs.at[mine], dev).start()
                    remote(l_send.at[dev], l_all.at[me], l_ss, l_rs.at[mine], dev).start()

                @pl.when(dev == me)
                def _():
                    pltpu.make_async_copy(o_send.at[dev], o_all.at[dev], o_rs.at[mine]).start()
                    pltpu.make_async_copy(l_send.at[dev], l_all.at[dev], l_rs.at[mine]).start()

        repeat(0, groups, body)

    repeat(1, blocks + 1, lambda b: emit(b - 1))

    highest, upper, lower = own_max, own_sum, own_total
    for r in range(blocks):
        part = pl.ds(r * kvh, kvh)
        settle(l_all.at[part], l_rs.at[r])
        spread = jnp.broadcast_to(l_all[part], (kvh, per, 128))

        def column(where):
            return jnp.sum(
                jnp.where(where[None], spread, 0.0), axis=-1, keepdims=True
            ).reshape(rows, 1)

        log = column(at_log)
        unit = column(at_unit)
        now = jnp.maximum(highest, log)
        keep, weight = jnp.exp(highest - now), jnp.exp(log - now)
        settle(o_all.at[part], o_rs.at[r])
        piece = o_all[part].astype(jnp.int32).astype(F32).reshape(rows, dim)
        upper = upper * keep + (weight * unit) * piece
        lower = lower * keep + weight
        highest = now
    result = upper / lower
    for h in range(kvh):
        for t in range(steps):
            at = h * per + t * gsize
            out_ref[t, h] = result[at:at + gsize]

    settle(q_all.at[pl.ds(0, n - 1)], q_ss)
    settle(others(k_all), k_ss)
    settle(others(v_all), v_ss)
    settle(o_all.at[pl.ds(0, n - 1)], o_ss)
    settle(l_all.at[pl.ds(0, n - 1)], l_ss)


def solution(mesh):
    n = mesh.shape["sample"]

    def shards(queries, pk, pv, sk, sv, lengths, nk, nv):
        _, steps, heads, dim = queries.shape
        tokens, kvh, _ = pk.shape
        gsize = heads // kvh
        suffix = sk.shape[1]
        per = steps * gsize
        group = math.gcd(kvh, 4)
        dma = pltpu.SemaphoreType.DMA
        out = pl.pallas_call(
            functools.partial(kernel, n, group),
            out_shape=jax.ShapeDtypeStruct((steps, kvh, gsize, dim), F32),
            in_specs=[pl.BlockSpec(memory_space=pltpu.SMEM)]
            + [pl.BlockSpec(memory_space=pltpu.HBM)] * 7,
            out_specs=pl.BlockSpec(memory_space=pltpu.VMEM),
            scratch_shapes=[
                pltpu.VMEM((steps, kvh, gsize, dim), BF16),
                pltpu.VMEM((tokens * kvh, dim), BF16),
                pltpu.VMEM((tokens * kvh, dim), BF16),
                pltpu.VMEM((tokens * kvh, dim), F32),
                pltpu.VMEM((kvh, tokens, dim), BF16),
                pltpu.VMEM((kvh, tokens, dim), BF16),
                pltpu.VMEM((n, steps, gsize, dim), BF16),
                pltpu.VMEM((kvh, tokens, dim), BF16),
                pltpu.VMEM((kvh, tokens, dim), BF16),
                pltpu.VMEM((kvh // 2, suffix, 2, dim), BF16),
                pltpu.VMEM((kvh // 2, suffix, 2, dim), BF16),
                pltpu.VMEM((steps, kvh, dim), BF16),
                pltpu.VMEM((steps, kvh, dim), BF16),
                pltpu.VMEM((kvh // 2, 2 * per, 2 * suffix), F32),
                pltpu.VMEM((2 * per, 2 * suffix), F32),
                pltpu.VMEM((n, steps, gsize, dim), I16),
                pltpu.VMEM((n, 1, 128), F32),
                pltpu.VMEM((n, steps, gsize, dim), I16),
                pltpu.VMEM((n, 1, 128), F32),
                pltpu.VMEM((n * per, kvh * tokens), BF16),
                pltpu.VMEM((n * per, kvh * tokens), BF16),
                pltpu.VMEM((n * per, 1), F32),
                pltpu.VMEM((n * per, 1), F32),
                dma((5,)), dma((kvh,)),
                pltpu.SemaphoreType.REGULAR, pltpu.SemaphoreType.REGULAR,
                dma, dma((n // kvh,)), dma, dma, dma, dma,
                dma, dma((n // kvh,)), dma, dma((n // kvh,)),
            ],
            compiler_params=pltpu.CompilerParams(
                collective_id=0, has_side_effects=True, vmem_limit_bytes=48 << 20
            ),
        )(lengths, *[pltpu.with_memory_space_constraint(x, pltpu.HBM) for x in (
            queries.reshape(steps, kvh, gsize, dim),
            pk.reshape(tokens * kvh, dim),
            pv.reshape(tokens * kvh, dim),
            sk.reshape(suffix, kvh // 2, 2, dim),
            sv.reshape(suffix, kvh // 2, 2, dim),
            nk.reshape(steps, kvh, dim),
            nv.reshape(steps, kvh, dim),
        )])
        return out.reshape(1, steps, heads, dim)

    spread = ("group", "sample")
    four = P(spread, None, None, None)
    three = P(spread, None, None)
    return jax.shard_map(
        shards, mesh=mesh,
        in_specs=(four, three, three, four, four, P(spread), four, four),
        out_specs=four, check_vma=False,
    )
```
